32 devices in a mesh: dp: 32 (over z, y, x, core).
Axes of the slice: x: 2, y: 2, z: 4, core: 2. Of those that a mesh axis runs over, the one named last changes fastest.
Arguments:
- text_states: bfloat16 [512, 16, 768], P('dp'), may hold values from -6 to 6
- text_len: int32 [512], P('dp'), may hold values from 1 to 16
- query_states: bfloat16 [512, 16, 768], P('dp'), may hold values from -6 to 6
- neg_owner: int32 [512, 2], P('dp'), may hold values from 0 to 31, all different within a row; in each aligned block of 16 rows (0 to 15, 16 to 31, ...) at most 2 rows name the same one
- neg_slot: int32 [512, 2], P('dp'), may hold values from 0 to 15
- projection_weight: bfloat16 [768, 2304], replicated, may hold values from -0.21875 to 0.21875
- output_weight: bfloat16 [768, 768], replicated, may hold values from -0.21875 to 0.21875
- ln_gain: float32 [768], replicated, may hold values from 0.5 to 1.5
- ln_bias: float32 [768], replicated, may hold values from -3 to 3
- itm_weight: float32 [768, 2], replicated, may hold values from -0.875 to 0.875
- itm_bias: float32 [2], replicated, may hold values from -3 to 3
Outputs:
- pair_logits: float32 [512, 3, 2], P('dp')
- grad_text: bfloat16 [512, 16, 768], P('dp')
- grad_query: bfloat16 [512, 16, 768], P('dp')
- grad_qkv: float32 [768, 2304], replicated
- grad_out: float32 [768, 768], replicated
The draws below stay inside these ranges and needn't reach their ends.
Inputs may be any that keep to these rules, and one draw needn't show every extreme that they name: `neg_owner`: the two negatives of a caption lie in different blocks; among the 16 captions of one device no block is named more than 2 times, and in some device exactly 2 times.
All inputs are finite; a program needn't handle non-finite values.
Results may differ from the reference program's by a relative error of at most 0.0075.
Values may be sent and summed in bfloat16 or wider, within the bound.
No kernel may reach another device: no remote copies, remote signals or barrier semaphores. Data moves between devices by JAX's collectives and lax.ppermute only.
A program may use at most 128 MiB of HBM per device.

```python
import math
import jax
import jax.numpy as jnp
import numpy as np
from jax import lax

D = 768
HEADS = 12
NQ = 16
L = 16
CAP = 2
P_DEV = 16
CAPTIONS = 512
N_DP = 32


def touch_ends(result, stream_key, least, top_value):
    longest = result.shape.index(max(result.shape))
    spots = []
    for shift in (0, 1):
        where = [jax.random.randint(jax.random.fold_in(stream_key, axis), (), 0, length) for axis, length in enumerate(result.shape)]
        where[longest] = (where[longest] + shift) % result.shape[longest]
        spots.append(tuple(where))
    return result.at[spots[0]].set(least).at[spots[1]].set(top_value)


def levels(stream_key, extent, shards, least, top_value):
    def one(axis_at, blocks):
        steps = jax.random.uniform(jax.random.fold_in(jax.random.fold_in(stream_key, 6), axis_at), (blocks,), jnp.float32, least / len(shards), top_value / len(shards))
        return jnp.repeat(jnp.exp(steps), extent[axis_at] // blocks).reshape((-1,) + (1,) * (len(extent) - axis_at - 1))

    level = one(*shards[0])
    for cut in shards[1:]:
        level = level * one(*cut)
    return level


def shared_out(own_key, own, number, rows, amount, top, limit, lean):
    ranking = jax.random.permutation(own_key, amount)
    crowded, ordinary = load_shares(amount, rows * top, limit, lean, True), load_shares(amount, rows * top, limit, lean, False)
    places = jnp.arange(amount)

    def named(sizes, offset_by):
        used = int((sizes > 0).sum())
        fixed = max(1, used // 4)
        passed = fixed + (places - fixed + offset_by * (used - fixed)) % max(1, amount - fixed)
        return jnp.zeros((amount,), jnp.int32).at[ranking[jnp.where(places < fixed, places, passed)]].set(jnp.asarray(sizes, jnp.int32))

    sizes = jnp.where(number % 4 == 0, named(crowded, number // 4), named(ordinary, number - number // 4 - 1))
    mixed = jax.random.permutation(jax.random.fold_in(own, 3), amount)
    giver, receiver = mixed[0:amount // 2 * 2:2], mixed[1:amount // 2 * 2:2]
    margin = jnp.minimum(sizes[giver] - 1, limit - sizes[receiver]) // 2
    margin = jnp.where((giver == ranking[0]) | (receiver == ranking[0]) | (sizes[receiver] == 0), 0, jnp.maximum(margin, 0))
    passed = jax.random.randint(jax.random.fold_in(own, 4), (amount // 2,), 0, 1 << 20) % (margin + 1)
    sizes = sizes.at[giver].add(-passed).at[receiver].add(passed)
    items = jnp.searchsorted(jnp.cumsum(sizes), jnp.arange(rows * top), side="right").astype(jnp.int32)
    grid = items.reshape(top, rows).T
    grid = grid[jax.random.permutation(jax.random.fold_in(own, 1), rows)]
    offset_by = jax.random.randint(jax.random.fold_in(own, 2), (rows, 1), 0, top)
    return jnp.take_along_axis(grid, (jnp.arange(top)[None, :] + offset_by) % top, axis=1)


def load_shares(number_of, total, most, slope, full):
    weights = [(1 << 20) // math.isqrt(rank ** slope) + 1 for rank in range(1, number_of + 1)]
    largest = most if full else min(most, max(-(-total // number_of), total * weights[0] // sum(weights)))
    least = 1 if total - largest >= number_of - 1 else 0
    holding, spare = [largest] + [least] * (number_of - 1), total - largest - least * (number_of - 1)
    while spare > 0:
        free = [i for i in range(1, number_of) if holding[i] < largest] or [i for i in range(1, number_of) if holding[i] < most]
        pool, budget = sum([weights[i] for i in free]), spare
        for i in free:
            extra = min(most - holding[i], max(1, budget * weights[i] // pool), spare)
            holding[i] = holding[i] + extra
            spare = spare - extra
    return np.array(holding)


def gaussian(stream_key, shape, scale, most, cuts=(), kind=jnp.bfloat16):
    entries = jax.random.normal(stream_key, shape, jnp.float32) * scale
    if len(cuts) > 0:
        entries = levels(stream_key, shape, cuts, -0.22, 0.18) * entries
    return jnp.clip(entries, min=-most, max=most).astype(kind)


def setup_inputs(seed: int = 0) -> dict:
    arg_keys = jax.random.split(jax.random.key(seed), 12)
    text_states = gaussian(arg_keys[0], (CAPTIONS, L, D), 1.0, 6.0, ((0, 32),))
    text_len = touch_ends(jax.random.randint(arg_keys[1], (CAPTIONS,), 1, L + 1), jax.random.fold_in(arg_keys[1], 1), 1, L).astype(jnp.int32)
    query_states = gaussian(arg_keys[2], (CAPTIONS, NQ, D), 1.0, 6.0, ((0, 32),))
    neg_owner_keys = jax.random.split(jax.random.fold_in(arg_keys[3], 1), CAPTIONS // P_DEV)
    neg_owner_turns = jax.random.permutation(jax.random.fold_in(arg_keys[3], 3), CAPTIONS // P_DEV)
    neg_owner = jax.vmap(lambda own, number: shared_out(jax.random.fold_in(arg_keys[3], 2), own, number, P_DEV, N_DP, 2, CAP, 2))(neg_owner_keys, neg_owner_turns).reshape((CAPTIONS, 2))
    neg_slot = touch_ends(jax.random.randint(arg_keys[4], (CAPTIONS, 2), 0, P_DEV), jax.random.fold_in(arg_keys[4], 1), 0, P_DEV - 1).astype(jnp.int32)
    projection_weight = gaussian(arg_keys[5], (D, 3 * D), D ** -0.5, 0.21875)
    output_weight = gaussian(arg_keys[6], (D, D), D ** -0.5, 0.21875)
    ln_gain = jnp.clip(1.0 + 0.1 * jax.random.normal(arg_keys[7], (D,), jnp.float32), 0.5, 1.5)
    ln_bias = gaussian(arg_keys[8], (D,), 0.5, 3.0, (), jnp.float32)
    itm_weight = gaussian(arg_keys[9], (D, 2), (D // 16) ** -0.5, 0.875, (), jnp.float32)
    itm_bias = gaussian(arg_keys[10], (2,), 1.0, 3.0, (), jnp.float32)
    return dict(text_states=text_states, text_len=text_len, query_states=query_states, neg_owner=neg_owner, neg_slot=neg_slot, projection_weight=projection_weight, output_weight=output_weight, ln_gain=ln_gain, ln_bias=ln_bias, itm_weight=itm_weight, itm_bias=itm_bias)


def matrix_product(einsum_form, left_side, right_side):
    return jnp.einsum(einsum_form, left_side.astype(jnp.float32), right_side.astype(jnp.float32), precision=lax.Precision.HIGHEST)

def split_heads(tensor, head_number):
    return tensor.reshape(tensor.shape[:-1] + (head_number, tensor.shape[-1] // head_number))

def merge_heads(tensor):
    return tensor.reshape(tensor.shape[0], tensor.shape[1], tensor.shape[2] * tensor.shape[3])

def tail_loss(hidden_states, ln_gain, ln_bias, itm_weight, itm_bias, labels):
    center = hidden_states - lax.optimization_barrier(jnp.mean(hidden_states, axis=-1, keepdims=True))
    spread = lax.optimization_barrier(jnp.mean(center * center, axis=-1, keepdims=True))
    normed = center * lax.rsqrt(spread + 1e-06) * ln_gain + ln_bias
    pooled = lax.optimization_barrier(jnp.mean(normed, axis=1))
    logits = jnp.dot(pooled, itm_weight, precision=lax.Precision.HIGHEST) + itm_bias
    losses = jax.nn.logsumexp(logits, axis=-1) - lax.optimization_barrier(jnp.sum(logits * labels, axis=-1))
    return (jnp.sum(losses), logits)

def pair_work(caption_rows, lengths, images, projection_weight, output_weight, ln_gain, ln_bias, itm_weight, itm_bias):
    caption_texts, text_rows, hidden_width = caption_rows.shape
    query_row_count = images.shape[2]
    pair_rows = caption_texts * 3
    head_number = HEADS
    score_scale = 1.0 / math.sqrt(hidden_width // head_number)
    text_kv = matrix_product('bld,de->ble', caption_rows, projection_weight[:, hidden_width:]).astype(jnp.bfloat16)
    image_row_count = images.reshape(pair_rows, query_row_count, hidden_width)
    image_projected = matrix_product('tns,sm->tnm', image_row_count, projection_weight).astype(jnp.bfloat16)
    text_wide = jnp.broadcast_to(text_kv[:, None], (caption_texts, 3, text_rows, 2 * hidden_width)).reshape(pair_rows, text_rows, 2 * hidden_width)
    queries = split_heads(image_projected[:, :, :hidden_width], head_number)
    key_heads = split_heads(jnp.concatenate([image_projected[:, :, hidden_width:2 * hidden_width], text_wide[:, :, :hidden_width]], axis=1), head_number)
    value_heads = split_heads(jnp.concatenate([image_projected[:, :, 2 * hidden_width:], text_wide[:, :, hidden_width:]], axis=1), head_number)
    position = jnp.arange(query_row_count + text_rows)
    key_valid = (position[None, :] < query_row_count) | (position[None, :] - query_row_count < lengths[:, None])
    key_valid = jnp.repeat(key_valid, 3, axis=0)
    scores = matrix_product('bqhe,bkhe->bhqk', queries, key_heads) * score_scale
    scores = jnp.where(key_valid[:, None, None, :], scores, -1e+30)
    shifted = jnp.exp(scores - lax.optimization_barrier(jnp.max(scores, axis=-1, keepdims=True)))
    weights = shifted / lax.optimization_barrier(jnp.sum(shifted, axis=-1, keepdims=True))
    weights_low = weights.astype(jnp.bfloat16)
    attended_context = merge_heads(matrix_product('bhqk,bkhe->bqhe', weights_low, value_heads).astype(jnp.bfloat16))
    hidden_states = image_row_count.astype(jnp.float32) + matrix_product('tns,sm->tnm', attended_context, output_weight)
    labels = jnp.tile(jnp.array([[0.0, 1.0], [1.0, 0.0], [1.0, 0.0]], dtype=jnp.float32), (caption_texts, 1))

    def loss_of(hidden_in):
        return tail_loss(hidden_in, ln_gain, ln_bias, itm_weight, itm_bias, labels)
    loss_total, pullback, logits = jax.vjp(loss_of, hidden_states, has_aux=True)
    hidden_gradient = pullback(jnp.ones_like(loss_total))[0]
    attention_gradient = hidden_gradient.astype(jnp.bfloat16)
    output_weight_gradient = matrix_product('nxv,nxl->vl', attended_context, attention_gradient)
    context_gradient = split_heads(matrix_product('kvp,mp->kvm', attention_gradient, output_weight).astype(jnp.bfloat16), head_number)
    grad_probs = matrix_product('bqhe,bkhe->bhqk', context_gradient, value_heads)
    grad_values = matrix_product('bhqk,bqhe->bkhe', weights_low, context_gradient)
    grad_scores = (weights * (grad_probs - lax.optimization_barrier(jnp.sum(grad_probs * weights, axis=-1, keepdims=True))) * score_scale).astype(jnp.bfloat16)
    grad_queries = merge_heads(matrix_product('bhqk,bkhe->bqhe', grad_scores, key_heads))
    grad_keys = merge_heads(matrix_product('bhqk,bqhe->bkhe', grad_scores, queries))
    grad_values = merge_heads(grad_values)
    image_projection_gradient = jnp.concatenate([grad_queries, grad_keys[:, :query_row_count], grad_values[:, :query_row_count]], axis=-1).astype(jnp.bfloat16)
    grad_text_kv = jnp.concatenate([grad_keys[:, query_row_count:], grad_values[:, query_row_count:]], axis=-1)
    grad_text_kv = lax.optimization_barrier(jnp.sum(grad_text_kv.reshape(caption_texts, 3, text_rows, 2 * hidden_width), axis=1)).astype(jnp.bfloat16)
    image_gradient = (matrix_product('kvp,mp->kvm', image_projection_gradient, projection_weight) + hidden_gradient).reshape(caption_texts, 3, query_row_count, hidden_width)
    grad_text = matrix_product('ble,de->bld', grad_text_kv, projection_weight[:, hidden_width:])
    projection_weight_gradient = matrix_product('nxv,nxl->vl', image_row_count, image_projection_gradient)
    projection_weight_gradient = projection_weight_gradient + jnp.pad(matrix_product('bld,ble->de', caption_rows, grad_text_kv), ((0, 0), (hidden_width, 0)))
    return (logits.reshape(caption_texts, 3, 2), grad_text, image_gradient, projection_weight_gradient, output_weight_gradient)

def reference(text_states, text_len, query_states, neg_owner, neg_slot, projection_weight, output_weight, ln_gain, ln_bias, itm_weight, itm_bias):
    all_pairs = text_states.shape[0]
    hidden_width = text_states.shape[2]
    query_row_count = query_states.shape[1]
    block_rows = math.gcd(all_pairs, 256)
    block_count = all_pairs // block_rows
    neg_image = (neg_owner * P_DEV + neg_slot).astype(jnp.int32)

    def visit_block(state_sum, inputs):
        neg_sum, sum_qkv, sum_out = state_sum
        caption_rows, lengths, own_images, chosen = inputs
        others = jnp.take(query_states, chosen.reshape(-1), axis=0).reshape(block_rows, 2, query_row_count, hidden_width)
        images = jnp.concatenate([own_images[:, None], others], axis=1)
        logits, grad_text, image_gradient, projection_weight_gradient, output_weight_gradient = pair_work(caption_rows, lengths, images, projection_weight, output_weight, ln_gain, ln_bias, itm_weight, itm_bias)
        rounded = lax.optimization_barrier(image_gradient[:, 1:].astype(jnp.bfloat16)).astype(jnp.float32)
        neg_sum = neg_sum.at[chosen.reshape(-1)].add(rounded.reshape(2 * block_rows, query_row_count, hidden_width))
        return ((neg_sum, sum_qkv + projection_weight_gradient, sum_out + output_weight_gradient), (logits, grad_text.astype(jnp.bfloat16), image_gradient[:, 0]))
    initial = (jnp.zeros((all_pairs, query_row_count, hidden_width), jnp.float32), jnp.zeros(projection_weight.shape, jnp.float32), jnp.zeros(output_weight.shape, jnp.float32))
    inputs = (text_states.reshape(block_count, block_rows, text_states.shape[1], hidden_width), text_len.reshape(block_count, block_rows), query_states.reshape(block_count, block_rows, query_row_count, hidden_width), neg_image.reshape(block_count, block_rows, 2))
    finals, stacked = lax.scan(visit_block, initial, inputs)
    neg_sum, sum_qkv, sum_out = finals
    logits, grad_text, grad_own = stacked
    grad_query = (grad_own.reshape(all_pairs, query_row_count, hidden_width) + neg_sum).astype(jnp.bfloat16)
    return (logits.reshape(all_pairs, 3, 2), grad_text.reshape(text_states.shape), grad_query, sum_qkv / all_pairs, sum_out / all_pairs)
```

```python
import functools
import jax
import jax.numpy as jnp
from jax import lax
from jax.experimental import pallas as pl
from jax.experimental.pallas import tpu as pltpu

from jax.sharding import PartitionSpec as P

BF = jnp.bfloat16
F32 = jnp.float32


def dot_nt(a, b):
    return lax.dot_general(a, b, (((1,), (1,)), ((), ())), preferred_element_type=F32)


def dot_nn(a, b):
    return lax.dot_general(a, b, (((1,), (0,)), ((), ())), preferred_element_type=F32)


def core_kernel(lens, x, qkv, tkv, wo, gain, bias, head_w, head_b, text_in, logits, gh, ga, ctx, dqkv, dtext, probs, dctx, *, negatives):
    rows, width = x.shape
    pairs_of_units = rows // 64
    quads = width // 256
    scale = 0.125
    lane = lax.broadcasted_iota(jnp.int32, (128, 128), 1)
    left = lane < 64
    lane32 = lax.broadcasted_iota(jnp.int32, (32, 128), 1)
    row32 = lax.broadcasted_iota(jnp.int32, (32, 128), 0)
    qg = row32 // 16
    uu = lane32 // 64
    key = lane32 % 64
    is_image = key < 32
    image_ok = is_image & ((key // 16) == qg)
    tg = (key - 32) // 16
    tpos = key % 16
    text_ok = jnp.logical_not(is_image) & (tg == (uu if negatives else qg))
    half32 = lane32 < 64
    hm_lane = lax.broadcasted_iota(jnp.int32, (1, 256), 1) // 64
    head_mask = [(hm_lane == h).astype(F32).astype(BF) for h in range(4)]
    zero64 = jnp.zeros((64, 256), BF)

    def head_blocks(t):
        return jnp.concatenate([t * m for m in head_mask], axis=0)

    def text_rows(j, u):
        if negatives:
            return pl.ds(pl.multiple_of(j * 32, 32), 32)
        return pl.ds(pl.multiple_of(j * 64 + u * 32, 32), 32)

    def unit_rows(j, u):
        return pl.ds(pl.multiple_of(j * 64 + u * 32, 32), 32)

    def stacked(j, part, q):
        cols = pl.ds(width * part + q * 256, 256)
        tcols = pl.ds(width * (part - 1) + q * 256, 256)
        both = []
        for u in range(2):
            t = jnp.concatenate([qkv[unit_rows(j, u), cols], tkv[text_rows(j, u), tcols]], axis=0)
            both.append(t)
        return jnp.concatenate(
            [jnp.concatenate([both[0], zero64], axis=1), jnp.concatenate([zero64, both[1]], axis=1)],
            axis=0,
        )

    def wide(ref, j, q):
        cols = pl.ds(q * 256, 256)
        return [head_blocks(ref[unit_rows(j, u), cols]) for u in range(2)]

    def gathered(full, u):
        parts = []
        for t in range(2):
            cols = slice(u * 256 + t * 128, u * 256 + t * 128 + 128)
            a = full[(2 * t) * 32 : (2 * t + 1) * 32, cols]
            b = full[(2 * t + 1) * 32 : (2 * t + 2) * 32, cols]
            parts.append(jnp.where(half32, a, b))
        return jnp.concatenate(parts, axis=1)

    def half_reduce(t, fill, op):
        a = op(jnp.where(left, t, fill), axis=1, keepdims=True)
        b = op(jnp.where(left, fill, t), axis=1, keepdims=True)
        return a, b

    def forward(j, carry):
        if negatives:
            n0 = lens[2 * j]
            n1 = lens[2 * j + 1]
            limit = jnp.where(uu == 0, n0, n1)
        else:
            n = [lens[4 * j + i] for i in range(4)]
            limit = jnp.where(
                uu == 0, jnp.where(qg == 0, n[0], n[1]), jnp.where(qg == 0, n[2], n[3])
            )
        valid32 = image_ok | (text_ok & (tpos < limit))
        valid32 = jnp.where(valid32, 1.0, 0.0)
        valid = jnp.concatenate([valid32] * 4, axis=0) > 0.5
        for q in range(quads):
            queries = wide(qkv, j, q)
            keys = stacked(j, 1, q)
            s = dot_nt(jnp.concatenate(queries, axis=1), keys) * scale
            s = jnp.where(valid, s, -1e30)
            m0, m1 = half_reduce(s, -3e38, jnp.max)
            e = jnp.exp(s - jnp.where(left, m0, m1))
            d0, d1 = half_reduce(e, 0.0, jnp.sum)
            p = e * jnp.where(left, 1.0 / d0, 1.0 / d1)
            probs[j, q] = p
            full = dot_nn(p.astype(BF), stacked(j, 2, q))
            for u in range(2):
                ctx[unit_rows(j, u), pl.ds(q * 256, 256)] = gathered(full, u).astype(BF)
        return carry

    lax.fori_loop(0, pairs_of_units, forward, 0)

    chunk = 128
    w0 = head_w[0:1, :]
    w1 = head_w[1:2, :]

    def middle(i, carry):
        rs = pl.ds(pl.multiple_of(i * chunk, chunk), chunk)
        hid = x[rs, :].astype(F32) + dot_nn(ctx[rs, :], wo[...])
        cen = hid - jnp.mean(hid, axis=1, keepdims=True)
        spread = jnp.mean(cen * cen, axis=1, keepdims=True)
        inv = lax.rsqrt(spread + 1e-06)
        xhat = cen * inv
        pooled = jnp.sum(xhat.reshape(chunk // 16, 16, width), axis=1) * (1.0 / 16.0)
        pooled = pooled * gain[...] + bias[...]
        l0 = jnp.sum(pooled * w0, axis=1, keepdims=True) + head_b[0]
        l1 = jnp.sum(pooled * w1, axis=1, keepdims=True) + head_b[1]
        cols = lax.broadcasted_iota(jnp.int32, (chunk // 16, 128), 1)
        logits[pl.ds(pl.multiple_of(i * (chunk // 16), chunk // 16), chunk // 16), :] = jnp.where(
            cols == 0, l0, l1
        )
        top = jnp.maximum(l0, l1)
        e0 = jnp.exp(l0 - top)
        e1 = jnp.exp(l1 - top)
        wrong = (e1 if negatives else e0) / (e0 + e1)
        slope = (w1 - w0) if negatives else (w0 - w1)
        dx = (wrong * (1.0 / 16.0)) * slope * gain[...]
        mean_dx = jnp.mean(dx, axis=1, keepdims=True)
        dx = jnp.broadcast_to(dx[:, None, :], (chunk // 16, 16, width)).reshape(chunk, width)
        mean_dx = jnp.broadcast_to(mean_dx[:, None, :], (chunk // 16, 16, 1)).reshape(chunk, 1)
        along = jnp.mean(dx * xhat, axis=1, keepdims=True)
        g = inv * (dx - mean_dx - xhat * along)
        gh[rs, :] = g
        gl = g.astype(BF)
        ga[rs, :] = gl
        dctx[rs, :] = dot_nt(gl, wo[...]).astype(BF)
        return carry

    lax.fori_loop(0, rows // chunk, middle, 0)

    def backward(j, carry):
        for q in range(quads):
            p = probs[j, q]
            dc = wide(dctx, j, q)
            dp = dot_nt(jnp.concatenate(dc, axis=1), stacked(j, 2, q))
            r0, r1 = half_reduce(dp * p, 0.0, jnp.sum)
            ds = (p * (dp - jnp.where(left, r0, r1)) * scale).astype(BF)
            full = dot_nn(ds, stacked(j, 1, q))
            for u in range(2):
                dqkv[unit_rows(j, u), pl.ds(q * 256, 256)] = gathered(full, u).astype(BF)
            queries = wide(qkv, j, q)
            dst = ds.T
            pt = p.astype(BF).T
            for part, lhs, rhs in ((1, dst, queries), (2, pt, dc)):
                outs = [dot_nn(lhs[u * 64 : u * 64 + 64], rhs[u]) for u in range(2)]
                for u in range(2):
                    dqkv[unit_rows(j, u), pl.ds(width * part + q * 256, 256)] = outs[u][:32].astype(BF)
                tcols = pl.ds(width * (part - 1) + q * 256, 256)
                if negatives:
                    tr = text_rows(j, 0)
                    total = text_in[tr, tcols] + outs[0][32:] + outs[1][32:]
                    dtext[tr, tcols] = total.astype(BF)
                else:
                    for u in range(2):
                        dtext[text_rows(j, u), tcols] = outs[u][32:]
        return carry

    lax.fori_loop(0, pairs_of_units, backward, 0)


def pair_core(negatives, lens, x, qkv, tkv, wo, gain, bias, head_w, head_b, text_in):
    rows, width = x.shape
    text_n = tkv.shape[0]
    body = functools.partial(core_kernel, negatives=negatives)
    if not negatives:
        def body(*refs):
            core_kernel(*refs[:9], None, *refs[9:], negatives=False)
    vm = pl.BlockSpec(memory_space=pltpu.VMEM)
    sm = pl.BlockSpec(memory_space=pltpu.SMEM)
    ins = [lens, x, qkv, tkv, wo, gain, bias, head_w, head_b]
    specs = [sm, vm, vm, vm, vm, vm, vm, vm, sm]
    if negatives:
        ins.append(text_in)
        specs.append(vm)
    out = [
        jax.ShapeDtypeStruct((rows // 16, 128), F32),
        jax.ShapeDtypeStruct((rows, width), F32),
        jax.ShapeDtypeStruct((rows, width), BF),
        jax.ShapeDtypeStruct((rows, width), BF),
        jax.ShapeDtypeStruct((rows, 3 * width), BF),
        jax.ShapeDtypeStruct((text_n, 2 * width), BF if negatives else F32),
    ]
    return pl.pallas_call(
        body,
        out_shape=out,
        in_specs=specs,
        out_specs=[vm] * len(out),
        scratch_shapes=[
            pltpu.VMEM((rows // 64, width // 256, 128, 128), F32),
            pltpu.VMEM((rows, width), BF),
        ],
        name="pair_core_neg" if negatives else "pair_core_pos",
        compiler_params=pltpu.CompilerParams(vmem_limit_bytes=48 * 1024 * 1024),
    )(*ins)


def grid_of(mesh):
    flat = list(mesh.devices.flat)
    sizes = [len({d.coords[a] for d in flat}) for a in range(3)]
    cores = len(flat) // (sizes[0] * sizes[1] * sizes[2])
    dims, stride = [], 1
    for s in [cores] + sizes:
        dims.append((stride, s))
        stride *= s
    return dims

def coord(dim):
    return (lax.axis_index("dp") // dim[0]) % dim[1]

def shifted(x, dim, k, n):
    stride, size = dim
    table = []
    for i in range(n):
        c = (i // stride) % size
        table.append((i, i + ((c + k) % size - c) * stride))
    return lax.ppermute(x, "dp", table)

def pick(x, dim, k):
    return lax.dynamic_index_in_dim(x, (coord(dim) + k) % dim[1], 0, keepdims=False)

def scatter_sum(x, dim, n):
    size = dim[1]
    if size == 1: return x
    parts = x.reshape((size, x.shape[0] // size) + x.shape[1:])
    got = [shifted(pick(parts, dim, k).astype(BF), dim, k, n) for k in range(1, size)]
    total = pick(parts, dim, 0).astype(F32)
    for g in got: total = total + g.astype(F32)
    return total.astype(BF)

def gather_rows(x, dim, n):
    size = dim[1]
    if size == 1: return x
    out = jnp.zeros((size,) + x.shape, x.dtype)
    out = lax.dynamic_update_index_in_dim(out, x, coord(dim), 0)
    for k in range(1, size):
        out = lax.dynamic_update_index_in_dim(out, shifted(x, dim, k, n), (coord(dim) - k) % size, 0)
    return out.reshape((size * x.shape[0],) + x.shape[1:])

def reduce_all(xs, orders, n):
    xs = list(xs)
    depth = len(orders[0])
    for s in range(depth):
        xs = [scatter_sum(x, o[s], n) for x, o in zip(xs, orders)]
    for s in reversed(range(depth)):
        xs = [gather_rows(x, o[s], n) for x, o in zip(xs, orders)]
    return xs


CAP = 2


def dot_tn(a, b):
    return lax.dot_general(a, b, (((0,), (0,)), ((), ())), preferred_element_type=F32)


def on_device(
    text_states,
    text_len,
    query_states,
    neg_owner,
    neg_slot,
    projection_weight,
    output_weight,
    ln_gain,
    ln_bias,
    itm_weight,
    itm_bias,
    *,
    dims,
):
    captions, text_rows, width = text_states.shape
    image_rows = query_states.shape[1]
    peers = lax.axis_size("dp")
    flat_owner = neg_owner.reshape(-1)
    flat_slot = neg_slot.reshape(-1)
    requests = flat_owner.shape[0]
    ids = jnp.arange(requests)
    same_owner = flat_owner[:, None] == flat_owner[None, :]
    before = ids[:, None] > ids[None, :]
    rank = jnp.sum((same_owner & before).astype(jnp.int32), axis=1)
    bucket = flat_owner * CAP + rank
    slot_hot = bucket[:, None] == jnp.arange(peers * CAP)[None, :]
    wanted = jnp.sum(jnp.where(slot_hot, flat_slot[:, None] + 1, 0), axis=0).reshape(peers, CAP)
    requested = lax.all_to_all(wanted, "dp", split_axis=0, concat_axis=0, tiled=True)
    send_select = (requested.reshape(-1)[:, None] == jnp.arange(captions)[None, :] + 1).astype(BF)
    outgoing = jnp.dot(send_select, query_states.reshape(captions, -1), preferred_element_type=F32)
    outgoing = outgoing.astype(BF).reshape(peers, CAP, image_rows, width)
    fetched = lax.all_to_all(outgoing, "dp", split_axis=0, concat_axis=0, tiled=True)
    take_select = slot_hot.astype(BF)

    text = text_states.reshape(captions * text_rows, width)
    own = query_states.reshape(captions * image_rows, width)
    gain = ln_gain[None]
    bias = ln_bias[None]
    head_w = itm_weight.T
    text_kv = dot_nn(text, projection_weight[:, width:]).astype(BF)
    own_qkv = dot_nn(own, projection_weight).astype(BF)
    own_logits, own_gh, own_ga, own_ctx, own_dqkv, own_dtext = pair_core(
        False, text_len, own, own_qkv, text_kv, output_weight, gain, bias, head_w, itm_bias, None
    )
    own_grad = dot_nt(own_dqkv, projection_weight) + own_gh

    negatives = jnp.dot(
        take_select, fetched.reshape(peers * CAP, -1), preferred_element_type=F32
    ).astype(BF)
    others = negatives.reshape(requests * image_rows, width)
    neg_qkv = dot_nn(others, projection_weight).astype(BF)
    neg_logits, neg_gh, neg_ga, neg_ctx, neg_dqkv, dtext = pair_core(
        True,
        text_len,
        others,
        neg_qkv,
        text_kv,
        output_weight,
        gain,
        bias,
        head_w,
        itm_bias,
        own_dtext,
    )
    neg_grad = (dot_nt(neg_dqkv, projection_weight) + neg_gh).astype(BF)
    outgoing_grads = jnp.dot(
        take_select.T, neg_grad.reshape(requests, -1), preferred_element_type=F32
    ).astype(BF)
    outgoing_grads = outgoing_grads.reshape(peers, CAP, image_rows, width)
    returned = lax.all_to_all(outgoing_grads, "dp", split_axis=0, concat_axis=0, tiled=True)

    d_out = dot_tn(own_ctx, own_ga) + dot_tn(neg_ctx, neg_ga)
    d_kv = dot_tn(text, dtext)
    d_qkv = dot_tn(own, own_dqkv) + dot_tn(others, neg_dqkv)
    grad_text = dot_nt(dtext, projection_weight[:, width:]).astype(BF)

    core_dim, x_dim, y_dim, z_dim = dims
    first = (core_dim, x_dim, y_dim, z_dim)
    second = (core_dim, y_dim, x_dim, z_dim)
    half = width + width // 2
    parts = [
        jnp.concatenate([d_qkv[:, :width], d_qkv[:, width : 2 * width] + d_kv[:, :width]], axis=1),
        jnp.concatenate([d_qkv[:, 2 * width :] + d_kv[:, width:], d_out], axis=1),
    ]
    summed = reduce_all(parts, [first, second], peers)
    summed = [s.astype(F32) * (1.0 / (captions * peers)) for s in summed]
    sum_qkv = jnp.concatenate([summed[0], summed[1][:, :width]], axis=1)
    sum_out = summed[1][:, width:]

    received = jnp.dot(
        send_select.T, returned.reshape(peers * CAP, -1), preferred_element_type=F32
    )
    grad_query = (
        own_grad.reshape(captions, image_rows, width)
        + received.reshape(captions, image_rows, width)
    ).astype(BF)
    logits = jnp.concatenate(
        [own_logits[:, None, :2], neg_logits[:, :2].reshape(captions, 2, 2)], axis=1
    )
    return (
        logits,
        grad_text.reshape(captions, text_rows, width),
        grad_query,
        sum_qkv,
        sum_out,
    )


def solution(mesh):
    dims = grid_of(mesh)
    placed = (
        P("dp", None, None),
        P("dp"),
        P("dp", None, None),
        P("dp", None),
        P("dp", None),
        P(),
        P(),
        P(),
        P(),
        P(),
        P(),
    )
    return jax.shard_map(
        functools.partial(on_device, dims=dims),
        mesh=mesh,
        in_specs=placed,
        out_specs=(P("dp", None, None), P("dp", None, None), P("dp", None, None), P(), P()),
        check_vma=False,
    )
```

```python
import functools
import jax
import jax.numpy as jnp
from jax import lax
from jax.experimental import pallas as pl
from jax.experimental.pallas import tpu as pltpu

from jax.sharding import PartitionSpec as P


BF = jnp.bfloat16
F32 = jnp.float32


def dot_nt(a, b):
    return lax.dot_general(a, b, (((1,), (1,)), ((), ())), preferred_element_type=F32)


def dot_nn(a, b):
    return lax.dot_general(a, b, (((1,), (0,)), ((), ())), preferred_element_type=F32)


def core_kernel(lens, source, w_h, tkv, wo_h, gain, bias, head_w, head_b, text_h, place, logits, x_h, ga_h, ctx_h, dqkv_h, dtext_h, back_h, qkv, probs, dctx, gh, w, wo, text_in, x, ga, ctx, dqkv, dtext, back, sem_in, sem_out, sem_rows, *, positive):
    rows, width = ctx.shape
    loads = [
        pltpu.make_async_copy(
            w_h.at[:, pl.ds(n * width, width)], w.at[:, pl.ds(n * width, width)], sem_in.at[n]
        )
        for n in range(3)
    ]
    loads.append(pltpu.make_async_copy(wo_h, wo, sem_in.at[3]))
    if not positive:
        loads.append(pltpu.make_async_copy(text_h, text_in, sem_in.at[4]))
    for load in loads:
        load.start()
    saves = []

    def save(src, dst):
        copy = pltpu.make_async_copy(src, dst, sem_out.at[len(saves)])
        copy.start()
        saves.append(copy)

    pairs_of_units = rows // 64
    quads = width // 256
    scale = 0.125
    lane = lax.broadcasted_iota(jnp.int32, (128, 128), 1)
    left = lane < 64
    lane32 = lax.broadcasted_iota(jnp.int32, (32, 128), 1)
    row32 = lax.broadcasted_iota(jnp.int32, (32, 128), 0)
    qg = row32 // 16
    uu = lane32 // 64
    key = lane32 % 64
    is_image = key < 32
    image_ok = is_image & ((key // 16) == qg)
    tg = (key - 32) // 16
    tpos = key % 16
    text_ok = jnp.logical_not(is_image) & (tg == qg)
    half32 = lane32 < 64
    hm_lane = lax.broadcasted_iota(jnp.int32, (1, 256), 1) // 64
    head_mask = [(hm_lane == h).astype(F32).astype(BF) for h in range(4)]
    zero64 = jnp.zeros((64, 256), BF)

    def head_blocks(t):
        return jnp.concatenate([t * m for m in head_mask], axis=0)

    def unit_rows(j, u):
        return pl.ds(pl.multiple_of(j * 64 + u * 32, 32), 32)

    def stacked(j, part, q):
        cols = pl.ds(width * part + q * 256, 256)
        tcols = pl.ds(width * (part - 1) + q * 256, 256)
        both = []
        for u in range(2):
            t = jnp.concatenate([qkv[unit_rows(j, u), cols], tkv[unit_rows(j, u), tcols]], axis=0)
            both.append(t)
        return jnp.concatenate(
            [jnp.concatenate([both[0], zero64], axis=1), jnp.concatenate([zero64, both[1]], axis=1)],
            axis=0,
        )

    def wide(ref, j, q):
        cols = pl.ds(q * 256, 256)
        return [head_blocks(ref[unit_rows(j, u), cols]) for u in range(2)]

    def gathered(full, u):
        parts = []
        for t in range(2):
            cols = slice(u * 256 + t * 128, u * 256 + t * 128 + 128)
            a = full[(2 * t) * 32 : (2 * t + 1) * 32, cols]
            b = full[(2 * t + 1) * 32 : (2 * t + 2) * 32, cols]
            parts.append(jnp.where(half32, a, b))
        return jnp.concatenate(parts, axis=1)

    def half_reduce(t, fill, op):
        a = op(jnp.where(left, t, fill), axis=1, keepdims=True)
        b = op(jnp.where(left, fill, t), axis=1, keepdims=True)
        return a, b

    def forward(j, carry):
        n = [lens[4 * j + i] for i in range(4)]
        limit = jnp.where(
            uu == 0, jnp.where(qg == 0, n[0], n[1]), jnp.where(qg == 0, n[2], n[3])
        )
        valid32 = image_ok | (text_ok & (tpos < limit))
        valid32 = jnp.where(valid32, 1.0, 0.0)
        valid = jnp.concatenate([valid32] * 4, axis=0) > 0.5
        for q in range(quads):
            queries = wide(qkv, j, q)
            keys = stacked(j, 1, q)
            s = dot_nt(jnp.concatenate(queries, axis=1), keys) * scale
            s = jnp.where(valid, s, -1e30)
            m0, m1 = half_reduce(s, -3e38, jnp.max)
            e = jnp.exp(s - jnp.where(left, m0, m1))
            d0, d1 = half_reduce(e, 0.0, jnp.sum)
            p = e * jnp.where(left, 1.0 / d0, 1.0 / d1)
            probs[j, q] = p
            full = dot_nn(p.astype(BF), stacked(j, 2, q))
            for u in range(2):
                ctx[unit_rows(j, u), pl.ds(q * 256, 256)] = gathered(full, u).astype(BF)
        return carry

    if positive:
        x = source
    else:
        for i in range(rows // 16):
            x[i * 16 : i * 16 + 16, :] = source[pl.ds(pl.multiple_of(place[i] * 16, 16), 16), :]
        save(x, x_h)

    def project(n, carry):
        cols = pl.ds(pl.multiple_of(n * 256, 256), 256)
        qkv[:, cols] = dot_nn(x[...], w[:, cols]).astype(BF)
        return carry

    per = width // 256
    for n in range(3):
        loads[n].wait()
        lax.fori_loop(n * per, (n + 1) * per, project, 0)
    lax.fori_loop(0, pairs_of_units, forward, 0)
    save(ctx, ctx_h)
    loads[3].wait()

    chunk = 128
    w0 = head_w[0:1, :]
    w1 = head_w[1:2, :]

    def middle(i, carry):
        rs = pl.ds(pl.multiple_of(i * chunk, chunk), chunk)
        hid = x[rs, :].astype(F32) + dot_nn(ctx[rs, :], wo[...])
        cen = hid - jnp.mean(hid, axis=1, keepdims=True)
        spread = jnp.mean(cen * cen, axis=1, keepdims=True)
        inv = lax.rsqrt(spread + 1e-06)
        xhat = cen * inv
        pooled = jnp.sum(xhat.reshape(chunk // 16, 16, width), axis=1) * (1.0 / 16.0)
        pooled = pooled * gain[...] + bias[...]
        l0 = jnp.sum(pooled * w0, axis=1, keepdims=True) + head_b[0]
        l1 = jnp.sum(pooled * w1, axis=1, keepdims=True) + head_b[1]
        cols = lax.broadcasted_iota(jnp.int32, (chunk // 16, 128), 1)
        logits[pl.ds(pl.multiple_of(i * (chunk // 16), chunk // 16), chunk // 16), :] = jnp.where(
            cols == 0, l0, l1
        )
        top = jnp.maximum(l0, l1)
        e0 = jnp.exp(l0 - top)
        e1 = jnp.exp(l1 - top)
        wrong = (e0 if positive else e1) / (e0 + e1)
        slope = (w0 - w1) if positive else (w1 - w0)
        dx = (wrong * (1.0 / 16.0)) * slope * gain[...]
        mean_dx = jnp.mean(dx, axis=1, keepdims=True)
        dx = jnp.broadcast_to(dx[:, None, :], (chunk // 16, 16, width)).reshape(chunk, width)
        mean_dx = jnp.broadcast_to(mean_dx[:, None, :], (chunk // 16, 16, 1)).reshape(chunk, 1)
        along = jnp.mean(dx * xhat, axis=1, keepdims=True)
        g = inv * (dx - mean_dx - xhat * along)
        gh[rs, :] = g
        gl = g.astype(BF)
        ga[rs, :] = gl
        dctx[rs, :] = dot_nt(gl, wo[...]).astype(BF)
        return carry

    lax.fori_loop(0, rows // chunk, middle, 0)
    save(ga, ga_h)
    if not positive:
        loads[4].wait()

    def row_copies(j):
        rs = pl.ds(pl.multiple_of(j * 64, 64), 64)
        return [
            pltpu.make_async_copy(dqkv.at[rs, :], dqkv_h.at[rs, :], sem_rows.at[0, j]),
            pltpu.make_async_copy(dtext.at[rs, :], dtext_h.at[rs, :], sem_rows.at[1, j]),
        ]

    def backward(j, carry):
        for q in range(quads):
            p = probs[j, q]
            dc = wide(dctx, j, q)
            dp = dot_nt(jnp.concatenate(dc, axis=1), stacked(j, 2, q))
            r0, r1 = half_reduce(dp * p, 0.0, jnp.sum)
            ds = (p * (dp - jnp.where(left, r0, r1)) * scale).astype(BF)
            full = dot_nn(ds, stacked(j, 1, q))
            for u in range(2):
                dqkv[unit_rows(j, u), pl.ds(q * 256, 256)] = gathered(full, u).astype(BF)
            queries = wide(qkv, j, q)
            dst = ds.T
            pt = p.astype(BF).T
            for part, lhs, rhs in ((1, dst, queries), (2, pt, dc)):
                outs = [dot_nn(lhs[u * 64 : u * 64 + 64], rhs[u]) for u in range(2)]
                for u in range(2):
                    dqkv[unit_rows(j, u), pl.ds(width * part + q * 256, 256)] = outs[u][:32].astype(BF)
                tcols = pl.ds(width * (part - 1) + q * 256, 256)
                for u in range(2):
                    total = outs[u][32:]
                    if not positive:
                        total = total + text_in[unit_rows(j, u), tcols]
                    dtext[unit_rows(j, u), tcols] = total.astype(dtext.dtype)
        for copy in row_copies(j):
            copy.start()
        return carry

    lax.fori_loop(0, pairs_of_units, backward, 0)

    def images(n, carry):
        cols = pl.ds(pl.multiple_of(n * 256, 256), 256)
        g = dot_nt(dqkv[...], w[cols, :]) + gh[:, cols]
        if positive:
            back[:, cols] = g
        else:
            gh[:, cols] = g
        return carry

    lax.fori_loop(0, width // 256, images, 0)
    if not positive:
        back[...] = jnp.zeros(back.shape, BF)
        for i in range(rows // 16):
            at = pl.ds(pl.multiple_of(place[i] * 16, 16), 16)
            back[at, :] = gh[i * 16 : i * 16 + 16, :].astype(BF)
    save(back, back_h)
    for j in range(pairs_of_units):
        for copy in row_copies(j):
            copy.wait()
    for copy in saves:
        copy.wait()


def pair_core(text_type, lens, source, w, tkv, wo, gain, bias, head_w, head_b, text_in, place):
    rows, width = tkv.shape[0], wo.shape[0]
    positive = place is None
    vm = pl.BlockSpec(memory_space=pltpu.VMEM)
    sm = pl.BlockSpec(memory_space=pltpu.SMEM)
    far = pl.BlockSpec(memory_space=pl.ANY)
    ins = [lens, source, w, tkv, wo, gain, bias, head_w, head_b]
    specs = [sm, vm, far, vm, far, vm, vm, vm, sm]
    if not positive:
        ins += [text_in, place]
        specs += [far, sm]
    back_type = F32 if positive else BF
    shapes = [
        ((rows, width), BF),
        ((rows, width), BF),
        ((rows, width), BF),
        ((rows, 3 * width), BF),
        ((rows, 2 * width), text_type),
        (source.shape, back_type),
    ]
    out = [jax.ShapeDtypeStruct((rows // 16, 128), F32)]
    out += [jax.ShapeDtypeStruct(s, t) for s, t in shapes]
    if positive:
        del out[1]

    def body(*refs):
        if positive:
            refs = refs[:9] + (None, None, refs[9], None) + refs[10:]
        core_kernel(*refs, positive=positive)

    units = rows // 64
    result = pl.pallas_call(
        body,
        out_shape=out,
        in_specs=specs,
        out_specs=[vm] + [far] * (len(out) - 1),
        scratch_shapes=[
            pltpu.VMEM((rows, 3 * width), BF),
            pltpu.VMEM((units, width // 256, 128, 128), F32),
            pltpu.VMEM((rows, width), BF),
            pltpu.VMEM((rows, width), F32),
            pltpu.VMEM(w.shape, BF),
            pltpu.VMEM(wo.shape, BF),
            pltpu.VMEM((rows, 2 * width), F32),
            *[pltpu.VMEM(s, t) for s, t in shapes],
            pltpu.SemaphoreType.DMA((5,)),
            pltpu.SemaphoreType.DMA((4,)),
            pltpu.SemaphoreType.DMA((2, units)),
        ],
        name="pair_core",
        compiler_params=pltpu.CompilerParams(vmem_limit_bytes=56 * 1024 * 1024),
    )(*ins)
    if positive:
        return [result[0], source] + list(result[1:])
    return result


def give_kernel(wanted, images, first, second):
    for p in range(first.shape[0] // 16):
        for s, out in enumerate((first, second)):
            at = jnp.maximum(wanted[p, s] - 1, 0)
            out[p * 16 : p * 16 + 16, :] = images[pl.ds(pl.multiple_of(at * 16, 16), 16), :]


def give(wanted, images):
    vm = pl.BlockSpec(memory_space=pltpu.VMEM)
    shape = jax.ShapeDtypeStruct((wanted.shape[0] * 16, images.shape[1]), BF)
    return pl.pallas_call(
        give_kernel,
        out_shape=[shape, shape],
        in_specs=[pl.BlockSpec(memory_space=pltpu.SMEM), vm],
        out_specs=[vm, vm],
        name="give",
    )(wanted, images)


def receive_kernel(wanted, own, first, second, out, total):
    total[...] = own[...]
    for s, part in enumerate((first, second)):

        def add(p, carry):
            at = wanted[p, s]

            @pl.when(at > 0)
            def _():
                rows = pl.ds(pl.multiple_of((at - 1) * 16, 16), 16)
                src = part[pl.ds(pl.multiple_of(p * 16, 16), 16), :]
                total[rows, :] = total[rows, :] + src.astype(F32)

            return carry

        lax.fori_loop(0, first.shape[0] // 16, add, 0)
    out[...] = total[...].astype(BF)


def receive(wanted, own, first, second):
    vm = pl.BlockSpec(memory_space=pltpu.VMEM)
    return pl.pallas_call(
        receive_kernel,
        out_shape=jax.ShapeDtypeStruct(own.shape, BF),
        in_specs=[pl.BlockSpec(memory_space=pltpu.SMEM), vm, vm, vm],
        out_specs=vm,
        scratch_shapes=[pltpu.VMEM(own.shape, F32)],
        name="receive",
    )(wanted, own, first, second)


def route_kernel(owner, slot, wanted, owners, color0):
    count = owner.shape[0]
    n = 2 * count
    peers = wanted.shape[0]
    o0, o1 = owner[:, 0:1], owner[:, 1:2]
    i = lax.broadcasted_iota(jnp.int32, (n, n), 0)
    k = lax.broadcasted_iota(jnp.int32, (n, n), 1)
    i_swap = jnp.where(i < count, i + count, i - count)
    k_swap = jnp.where(k < count, k + count, k - count)

    def row_of(col):
        return jnp.sum(jnp.where(i == k, col, 0), axis=0, keepdims=True)

    owner_col = jnp.concatenate([o0, o1], axis=0)
    swap_col = jnp.concatenate([o1, o0], axis=0)
    owner_row = row_of(owner_col)
    swap_row = row_of(swap_col)
    slot_row = row_of(jnp.concatenate([slot[:, 0:1], slot[:, 1:2]], axis=0))
    ahead = (owner_col == swap_row) & (i != k_swap)
    behind = (owner_row == swap_col) & (k != i_swap)
    reach = jnp.where(ahead | behind | (i == k), 1.0, 0.0)
    span = 1
    while span < count:
        low = reach.astype(BF)
        reach = jnp.where(dot_nn(low, low) > 0.5, 1.0, 0.0)
        span *= 2
    near = reach > 0.5
    first_row = jnp.min(jnp.where(near, i, n), axis=0, keepdims=True)
    second_row = jnp.min(jnp.where(near, i_swap, n), axis=0, keepdims=True)
    color_row = jnp.where(first_row < second_row, 0, 1)
    peer = lax.broadcasted_iota(jnp.int32, (peers, n), 0)
    asked = []
    for s in range(2):
        hit = (owner_row == peer) & (color_row == s)
        asked.append(jnp.sum(jnp.where(hit, slot_row + 1, 0), axis=1, keepdims=True))
    wanted[...] = jnp.concatenate(asked, axis=1)
    own_color = color_row[:, :count]
    swapped = owner_row[:, count:]
    straight = owner_row[:, :count]
    color0[...] = own_color
    owners[...] = jnp.concatenate(
        [jnp.where(own_color == 0, straight, swapped), jnp.where(own_color == 0, swapped, straight)],
        axis=0,
    )


def route(owner, slot, peers):
    vm = pl.BlockSpec(memory_space=pltpu.VMEM)
    count = owner.shape[0]
    return pl.pallas_call(
        route_kernel,
        out_shape=[
            jax.ShapeDtypeStruct((peers, 2), jnp.int32),
            jax.ShapeDtypeStruct((2, count), jnp.int32),
            jax.ShapeDtypeStruct((1, count), jnp.int32),
        ],
        in_specs=[vm, vm],
        out_specs=[vm, vm, vm],
        name="route",
    )(owner, slot)


def weight_kernel(core, *refs, flips, groups, with_text):
    xs = refs[:groups]
    ds = refs[groups : 2 * groups]
    rest = refs[2 * groups :]
    if with_text:
        text, dt = rest[:2]
        rest = rest[2:]
        lhs = xs + (text,)
    else:
        lhs = xs
    outs = rest[: len(flips)]
    turned = rest[len(flips) :]
    step = pl.program_id(0)
    rows_of, width = xs[0].shape
    half = width // 2
    per = width // 256
    for flip, out, hold in zip(flips, outs, turned):
        for part in range(2):

            @pl.when((step == 0) & ((core[0] + flip) % 2 == part))
            def _():
                col = 0
                for src in lhs:
                    for i in range(src.shape[0] // 128):
                        block = src[i * 128 : i * 128 + 128, part * half : (part + 1) * half]
                        hold[:, col : col + 128] = block.T
                        col += 128

        def columns(n, carry, more):
            cols = pl.ds(pl.multiple_of(n * 256, 256), 256)
            acc = dot_nn(hold[:, :rows_of], ds[0][:, cols])
            for g in range(1, groups):
                acc = acc + dot_nn(hold[:, g * rows_of : (g + 1) * rows_of], ds[g][:, cols])
            if more:
                acc = acc + dot_nn(hold[:, groups * rows_of :], dt[:, cols])
            out[:, cols] = acc.astype(BF)
            return carry

        if with_text:

            @pl.when(step == 0)
            def _():
                lax.fori_loop(0, per, functools.partial(columns, more=False), 0)

            @pl.when(step > 0)
            def _():
                lax.fori_loop(0, per, functools.partial(columns, more=True), 0)

        else:
            lax.fori_loop(0, per, functools.partial(columns, more=False), 0)


def weight_gradients(core, flips, xs, ds, text, dt):
    groups = len(xs)
    with_text = text is not None
    rows_of, width = xs[0].shape
    whole = lambda t: pl.BlockSpec(t.shape, lambda n, core: (0, 0))
    specs = [whole(x) for x in xs]
    specs += [pl.BlockSpec((rows_of, width), lambda n, core: (0, n)) for d in ds]
    arrays = [*xs, *ds]
    depth = groups * rows_of
    if with_text:
        arrays += [text, dt]
        specs.append(whole(text))
        specs.append(
            pl.BlockSpec((text.shape[0], width), lambda n, core: (0, jnp.maximum(n - 1, 0)))
        )
        depth += text.shape[0]
    half = width // 2
    return pl.pallas_call(
        functools.partial(weight_kernel, flips=flips, groups=groups, with_text=with_text),
        grid_spec=pltpu.PrefetchScalarGridSpec(
            num_scalar_prefetch=1,
            grid=(ds[0].shape[1] // width,),
            in_specs=specs,
            out_specs=[pl.BlockSpec((half, width), lambda n, core: (0, n))] * len(flips),
            scratch_shapes=[pltpu.VMEM((half, depth), BF)] * len(flips),
        ),
        out_shape=[jax.ShapeDtypeStruct((half, ds[0].shape[1]), BF)] * len(flips),
        name="weight_gradients",
        compiler_params=pltpu.CompilerParams(vmem_limit_bytes=56 * 1024 * 1024),
    )(core, *arrays)


def finish_kernel(at, part, *refs, factor):
    refs[-1][...] = part[...].astype(F32) * factor


def finish(at, part, rows, factor, before):
    count, total = part.shape
    steps = 2 if count % 32 == 0 else 1
    block = count // steps
    given = [] if before is None else [before]
    return pl.pallas_call(
        functools.partial(finish_kernel, factor=factor),
        grid_spec=pltpu.PrefetchScalarGridSpec(
            num_scalar_prefetch=1,
            grid=(steps,),
            in_specs=[pl.BlockSpec((block, total), lambda i, at: (i, 0))]
            + [pl.BlockSpec(memory_space=pl.ANY)] * len(given),
            out_specs=pl.BlockSpec((block, total), lambda i, at: (at[0] * steps + i, 0)),
        ),
        out_shape=jax.ShapeDtypeStruct((rows, total), F32),
        input_output_aliases={2: 0} if given else {},
        name="finish",
    )(at.reshape(1), part, *given)


def grid_of(mesh):
    flat = list(mesh.devices.flat)
    sizes = [len({d.coords[a] for d in flat}) for a in range(3)]
    dims, stride = [], 1
    for s in [len(flat) // (sizes[0] * sizes[1] * sizes[2])] + sizes:
        dims.append((stride, s))
        stride *= s
    return dims


def coord(dim):
    return (lax.axis_index("dp") // dim[0]) % dim[1]


def by_core(even, odd):
    if even == odd:
        return coord(even)
    return jnp.where(lax.axis_index("dp") % 2 == 0, coord(even), coord(odd))


def shifted(x, dims, k):
    n = lax.axis_size("dp")
    table = []
    for i in range(n):
        stride, size = dims[i % 2]
        c = (i // stride) % size
        table.append((i, i + ((c + k) % size - c) * stride))
    return lax.ppermute(x, "dp", table)


def total_of(terms):
    total = terms[0].astype(F32)
    for t in terms[1:]:
        total = total + t.astype(F32)
    return total


def scatter_terms(terms, dims):
    size = dims[0][1]
    at = by_core(*dims)
    split = [t.reshape((size, t.shape[0] // size) + t.shape[1:]) for t in terms]
    pick = lambda k: [
        lax.dynamic_index_in_dim(t, (at + k) % size, 0, keepdims=False) for t in split
    ]
    got = [shifted(total_of(pick(k)).astype(BF), dims, k) for k in range(1, size)]
    return pick(0) + got


def gather_rows(x, dims):
    size = dims[0][1]
    at = by_core(*dims)
    if size == 2:
        got = shifted(x, dims, 1)
        low = at == 0
        return jnp.concatenate([jnp.where(low, x, got), jnp.where(low, got, x)], axis=0)
    out = jnp.zeros((size,) + x.shape, x.dtype)
    out = lax.dynamic_update_index_in_dim(out, x, at, 0)
    for k in range(1, size):
        out = lax.dynamic_update_index_in_dim(out, shifted(x, dims, k), (at - k) % size, 0)
    return out.reshape((size * x.shape[0],) + x.shape[1:])


def step(
    text_states,
    text_len,
    query_states,
    neg_owner,
    neg_slot,
    projection_weight,
    output_weight,
    ln_gain,
    ln_bias,
    itm_weight,
    itm_bias,
    *,
    dims,
):
    captions, text_rows, width = text_states.shape
    image_rows = query_states.shape[1]
    peers = lax.axis_size("dp")
    wanted, owners, color = route(neg_owner, neg_slot, peers)
    requested = lax.all_to_all(wanted, "dp", split_axis=0, concat_axis=0, tiled=True)

    def exchange(t):
        split = t.reshape(peers, 1, image_rows, width)
        moved = lax.all_to_all(split, "dp", split_axis=0, concat_axis=0, tiled=True)
        return moved.reshape(t.shape)

    text = text_states.reshape(captions * text_rows, width)
    own = query_states.reshape(captions * image_rows, width)
    outgoing = give(requested, own)
    fetched = []
    for s in range(2):
        fetched.append(exchange(outgoing[s]))
    text_kv = dot_nn(text, projection_weight[:, width:]).astype(BF)
    results = []
    returned = []
    dtext = None
    for s in range(3):
        result = pair_core(
            BF if s == 2 else F32,
            text_len,
            own if s == 0 else fetched[s - 1],
            projection_weight,
            text_kv,
            output_weight,
            ln_gain[None],
            ln_bias[None],
            itm_weight.T,
            itm_bias,
            dtext,
            None if s == 0 else owners[s - 1],
        )
        results.append(result)
        dtext = result[5]
        if s > 0:
            returned.append(exchange(result[6]))

    rows = [r[1] for r in results]
    core = coord(dims[0]).reshape(1)
    core_dims = (dims[0], dims[0])
    x_dim, y_dim, z_dim = dims[1:]
    mixed = x_dim[1] == y_dim[1]
    flat_first = (x_dim, y_dim) if mixed else (x_dim, x_dim)
    flat_second = (y_dim, x_dim) if mixed else (y_dim, y_dim)
    deep = (z_dim, z_dim)
    factor = 1.0 / (captions * peers)

    keep_a, send_a = weight_gradients(
        core, (0, 1), [r[3] for r in results], [r[2] for r in results], None, None
    )
    a = [keep_a, shifted(send_a, core_dims, 1)]
    dqs = [r[4] for r in results]
    (send_b,) = weight_gradients(core, (1,), rows, dqs, text, dtext)
    got_b = shifted(send_b, core_dims, 1)
    (keep_b,) = weight_gradients(core, (0,), rows, dqs, text, dtext)
    b = [keep_b, got_b]
    grad_text = dot_nt(dtext, projection_weight[:, width:]).astype(BF)

    heads = [r[0][:, :2] for r in results]
    straight = color.reshape(captions, 1) == 0
    logits = jnp.stack(
        [
            heads[0],
            jnp.where(straight, heads[1], heads[2]),
            jnp.where(straight, heads[2], heads[1]),
        ],
        axis=1,
    )

    a = scatter_terms(a, deep)
    b = scatter_terms(b, flat_first)
    b = scatter_terms(b, flat_second)
    a = scatter_terms(a, flat_first)
    b = scatter_terms(b, deep)
    a = scatter_terms(a, flat_second)
    a = total_of(a).astype(BF)
    b = total_of(b).astype(BF)
    b = gather_rows(b, deep)
    a = gather_rows(a, flat_second)
    a = gather_rows(a, flat_first)
    b = gather_rows(b, flat_second)
    a = gather_rows(a, deep)
    other_a = shifted(a, core_dims, 1)
    size = flat_first[0][1]
    at = by_core(*flat_first)
    other_at = by_core(flat_first[1], flat_first[0])
    pieces = [(core[0] * size + at, b)]
    pieces.append(((1 - core[0]) * size + other_at, shifted(b, core_dims, 1)))
    for k in range(1, size):
        got = shifted(b, flat_first, k)
        pieces.append((core[0] * size + (at - k) % size, got))
        got = shifted(got, core_dims, 1)
        pieces.append(((1 - core[0]) * size + (other_at - k) % size, got))
    grad_query = receive(requested, results[0][6], *returned)
    sum_qkv = None
    for place, piece in pieces:
        sum_qkv = finish(place, piece, width, factor, sum_qkv)
    sum_out = finish(core[0], a, width, factor, None)
    sum_out = finish(1 - core[0], other_a, width, factor, sum_out)
    return (
        logits,
        grad_text.reshape(captions, text_rows, width),
        grad_query.reshape(captions, image_rows, width),
        sum_qkv,
        sum_out,
    )


def solution(mesh):
    dims = grid_of(mesh)
    placed = (
        P("dp", None, None),
        P("dp"),
        P("dp", None, None),
        P("dp", None),
        P("dp", None),
        P(),
        P(),
        P(),
        P(),
        P(),
        P(),
    )
    return jax.shard_map(
        functools.partial(step, dims=dims),
        mesh=mesh,
        in_specs=placed,
        out_specs=(P("dp", None, None), P("dp", None, None), P("dp", None, None), P(), P()),
        check_vma=False,
    )
```

```python
import functools
import jax
import jax.numpy as jnp
from jax import lax
from jax.experimental import pallas as pl
from jax.experimental.pallas import tpu as pltpu

from jax.sharding import PartitionSpec as P


BF = jnp.bfloat16
F32 = jnp.float32


def dot_nt(a, b):
    return lax.dot_general(a, b, (((1,), (1,)), ((), ())), preferred_element_type=F32)


def dot_nn(a, b):
    return lax.dot_general(a, b, (((1,), (0,)), ((), ())), preferred_element_type=F32)


def core_kernel(lens, source, w_h, tkv, wo_h, gain, bias, head_w, head_b, text_h, place, logits, x_h, ga_h, ctx_h, dqkv_h, dtext_h, back_h, qkv, probs, dctx, gh, w, wo, text_in, x, ga, ctx, dqkv, dtext, back, sem_in, sem_out, sem_rows, *, positive):
    rows, width = ctx.shape
    loads = [
        pltpu.make_async_copy(
            w_h.at[:, pl.ds(n * width, width)], w.at[:, pl.ds(n * width, width)], sem_in.at[n]
        )
        for n in range(3)
    ]
    loads.append(pltpu.make_async_copy(wo_h, wo, sem_in.at[3]))
    if not positive:
        loads.append(pltpu.make_async_copy(text_h, text_in, sem_in.at[4]))
    loads[0].start()
    loads[1].start()
    saves = []

    def save(src, dst):
        copy = pltpu.make_async_copy(src, dst, sem_out.at[len(saves)])
        copy.start()
        saves.append(copy)

    pairs_of_units = rows // 64
    quads = width // 256
    scale = 0.125
    lane = lax.broadcasted_iota(jnp.int32, (128, 128), 1)
    left = lane < 64
    lane32 = lax.broadcasted_iota(jnp.int32, (32, 128), 1)
    row32 = lax.broadcasted_iota(jnp.int32, (32, 128), 0)
    qg = row32 // 16
    uu = lane32 // 64
    key = lane32 % 64
    is_image = key < 32
    image_ok = is_image & ((key // 16) == qg)
    tg = (key - 32) // 16
    tpos = key % 16
    text_ok = jnp.logical_not(is_image) & (tg == qg)
    half32 = lane32 < 64
    hm_lane = lax.broadcasted_iota(jnp.int32, (1, 256), 1) // 64
    head_mask = [(hm_lane == h).astype(F32).astype(BF) for h in range(4)]
    zero64 = jnp.zeros((64, 256), BF)

    def head_blocks(t):
        return jnp.concatenate([t * m for m in head_mask], axis=0)

    def unit_rows(j, u):
        return pl.ds(pl.multiple_of(j * 64 + u * 32, 32), 32)

    def stacked(j, part, q):
        cols = pl.ds(width * part + q * 256, 256)
        tcols = pl.ds(width * (part - 1) + q * 256, 256)
        both = []
        for u in range(2):
            t = jnp.concatenate([qkv[unit_rows(j, u), cols], tkv[unit_rows(j, u), tcols]], axis=0)
            both.append(t)
        return jnp.concatenate(
            [jnp.concatenate([both[0], zero64], axis=1), jnp.concatenate([zero64, both[1]], axis=1)],
            axis=0,
        )

    def wide(ref, j, q):
        cols = pl.ds(q * 256, 256)
        return [head_blocks(ref[unit_rows(j, u), cols]) for u in range(2)]

    def gathered(full, u):
        parts = []
        for t in range(2):
            cols = slice(u * 256 + t * 128, u * 256 + t * 128 + 128)
            a = full[(2 * t) * 32 : (2 * t + 1) * 32, cols]
            b = full[(2 * t + 1) * 32 : (2 * t + 2) * 32, cols]
            parts.append(jnp.where(half32, a, b))
        return jnp.concatenate(parts, axis=1)

    def half_reduce(t, fill, op):
        a = op(jnp.where(left, t, fill), axis=1, keepdims=True)
        b = op(jnp.where(left, fill, t), axis=1, keepdims=True)
        return a, b

    def forward(j, carry):
        n = [lens[4 * j + i] for i in range(4)]
        limit = jnp.where(
            uu == 0, jnp.where(qg == 0, n[0], n[1]), jnp.where(qg == 0, n[2], n[3])
        )
        valid32 = image_ok | (text_ok & (tpos < limit))
        valid32 = jnp.where(valid32, 1.0, 0.0)
        valid = jnp.concatenate([valid32] * 4, axis=0) > 0.5
        for q in range(quads):
            queries = wide(qkv, j, q)
            keys = stacked(j, 1, q)
            s = dot_nt(jnp.concatenate(queries, axis=1), keys) * scale
            s = jnp.where(valid, s, -1e30)
            m0, m1 = half_reduce(s, -3e38, jnp.max)
            e = jnp.exp(s - jnp.where(left, m0, m1))
            d0, d1 = half_reduce(e, 0.0, jnp.sum)
            p = e * jnp.where(left, 1.0 / d0, 1.0 / d1)
            probs[j, q] = p
            full = dot_nn(p.astype(BF), stacked(j, 2, q))
            for u in range(2):
                ctx[unit_rows(j, u), pl.ds(q * 256, 256)] = gathered(full, u).astype(BF)
        return carry

    if positive:
        x = source
    else:
        for i in range(rows // 16):
            x[i * 16 : i * 16 + 16, :] = source[pl.ds(pl.multiple_of(place[i] * 16, 16), 16), :]
        save(x, x_h)

    def project(n, carry):
        cols = pl.ds(pl.multiple_of(n * 256, 256), 256)
        qkv[:, cols] = dot_nn(x[...], w[:, cols]).astype(BF)
        return carry

    per = width // 256
    for n in range(3):
        loads[n].wait()
        for load in loads[2:3] if n == 0 else loads[3:] if n == 1 else []:
            load.start()
        lax.fori_loop(n * per, (n + 1) * per, project, 0, unroll=3)
    lax.fori_loop(0, pairs_of_units, forward, 0, unroll=4)
    save(ctx, ctx_h)
    loads[3].wait()

    chunk = 128
    w0 = head_w[0:1, :]
    w1 = head_w[1:2, :]

    def middle(i, carry):
        rs = pl.ds(pl.multiple_of(i * chunk, chunk), chunk)
        hid = x[rs, :].astype(F32) + dot_nn(ctx[rs, :], wo[...])
        cen = hid - jnp.mean(hid, axis=1, keepdims=True)
        spread = jnp.mean(cen * cen, axis=1, keepdims=True)
        inv = lax.rsqrt(spread + 1e-06)
        xhat = cen * inv
        pooled = jnp.sum(xhat.reshape(chunk // 16, 16, width), axis=1) * (1.0 / 16.0)
        pooled = pooled * gain[...] + bias[...]
        l0 = jnp.sum(pooled * w0, axis=1, keepdims=True) + head_b[0]
        l1 = jnp.sum(pooled * w1, axis=1, keepdims=True) + head_b[1]
        cols = lax.broadcasted_iota(jnp.int32, (chunk // 16, 128), 1)
        logits[pl.ds(pl.multiple_of(i * (chunk // 16), chunk // 16), chunk // 16), :] = jnp.where(
            cols == 0, l0, l1
        )
        top = jnp.maximum(l0, l1)
        e0 = jnp.exp(l0 - top)
        e1 = jnp.exp(l1 - top)
        wrong = (e0 if positive else e1) / (e0 + e1)
        slope = (w0 - w1) if positive else (w1 - w0)
        dx = (wrong * (1.0 / 16.0)) * slope * gain[...]
        mean_dx = jnp.mean(dx, axis=1, keepdims=True)
        dx = jnp.broadcast_to(dx[:, None, :], (chunk // 16, 16, width)).reshape(chunk, width)
        mean_dx = jnp.broadcast_to(mean_dx[:, None, :], (chunk // 16, 16, 1)).reshape(chunk, 1)
        along = jnp.mean(dx * xhat, axis=1, keepdims=True)
        g = inv * (dx - mean_dx - xhat * along)
        gh[rs, :] = g
        gl = g.astype(BF)
        ga[rs, :] = gl
        dctx[rs, :] = dot_nt(gl, wo[...]).astype(BF)
        return carry

    lax.fori_loop(0, rows // chunk, middle, 0, unroll=2)
    save(ga, ga_h)
    if not positive:
        loads[4].wait()

    def row_copies(j):
        rs = pl.ds(pl.multiple_of(j * 64, 64), 64)
        return [
            pltpu.make_async_copy(dqkv.at[rs, :], dqkv_h.at[rs, :], sem_rows.at[0, j]),
            pltpu.make_async_copy(dtext.at[rs, :], dtext_h.at[rs, :], sem_rows.at[1, j]),
        ]

    def backward(j, carry):
        for q in range(quads):
            p = probs[j, q]
            dc = wide(dctx, j, q)
            dp = dot_nt(jnp.concatenate(dc, axis=1), stacked(j, 2, q))
            r0, r1 = half_reduce(dp * p, 0.0, jnp.sum)
            ds = (p * (dp - jnp.where(left, r0, r1)) * scale).astype(BF)
            full = dot_nn(ds, stacked(j, 1, q))
            for u in range(2):
                dqkv[unit_rows(j, u), pl.ds(q * 256, 256)] = gathered(full, u).astype(BF)
            queries = wide(qkv, j, q)
            dst = ds.T
            pt = p.astype(BF).T
            for part, lhs, rhs in ((1, dst, queries), (2, pt, dc)):
                outs = [dot_nn(lhs[u * 64 : u * 64 + 64], rhs[u]) for u in range(2)]
                for u in range(2):
                    dqkv[unit_rows(j, u), pl.ds(width * part + q * 256, 256)] = outs[u][:32].astype(BF)
                tcols = pl.ds(width * (part - 1) + q * 256, 256)
                for u in range(2):
                    total = outs[u][32:]
                    if not positive:
                        total = total + text_in[unit_rows(j, u), tcols]
                    dtext[unit_rows(j, u), tcols] = total.astype(dtext.dtype)
        for copy in row_copies(j):
            copy.start()
        return carry

    lax.fori_loop(0, pairs_of_units, backward, 0, unroll=2)

    def images(n, carry):
        cols = pl.ds(pl.multiple_of(n * 256, 256), 256)
        g = dot_nt(dqkv[...], w[cols, :]) + gh[:, cols]
        if positive:
            back[:, cols] = g
        else:
            gh[:, cols] = g
        return carry

    lax.fori_loop(0, width // 256, images, 0, unroll=3)
    if not positive:
        back[...] = jnp.zeros(back.shape, BF)
        for i in range(rows // 16):
            at = pl.ds(pl.multiple_of(place[i] * 16, 16), 16)
            back[at, :] = gh[i * 16 : i * 16 + 16, :].astype(BF)
    save(back, back_h)
    for j in range(pairs_of_units):
        for copy in row_copies(j):
            copy.wait()
    for copy in saves:
        copy.wait()


def pair_core(text_type, lens, source, w, tkv, wo, gain, bias, head_w, head_b, text_in, place):
    rows, width = tkv.shape[0], wo.shape[0]
    positive = place is None
    vm = pl.BlockSpec(memory_space=pltpu.VMEM)
    sm = pl.BlockSpec(memory_space=pltpu.SMEM)
    far = pl.BlockSpec(memory_space=pl.ANY)
    ins = [lens, source, w, tkv, wo, gain, bias, head_w, head_b]
    specs = [sm, vm, far, vm, far, vm, vm, vm, sm]
    if not positive:
        ins += [text_in, place]
        specs += [far, sm]
    back_type = F32 if positive else BF
    shapes = [
        ((rows, width), BF),
        ((rows, width), BF),
        ((rows, width), BF),
        ((rows, 3 * width), BF),
        ((rows, 2 * width), text_type),
        (source.shape, back_type),
    ]
    out = [jax.ShapeDtypeStruct((rows // 16, 128), F32)]
    out += [jax.ShapeDtypeStruct(s, t) for s, t in shapes]
    if positive:
        del out[1]

    def body(*refs):
        if positive:
            refs = refs[:9] + (None, None, refs[9], None) + refs[10:]
        core_kernel(*refs, positive=positive)

    units = rows // 64
    result = pl.pallas_call(
        body,
        out_shape=out,
        in_specs=specs,
        out_specs=[vm] + [far] * (len(out) - 1),
        scratch_shapes=[
            pltpu.VMEM((rows, 3 * width), BF),
            pltpu.VMEM((units, width // 256, 128, 128), F32),
            pltpu.VMEM((rows, width), BF),
            pltpu.VMEM((rows, width), F32),
            pltpu.VMEM(w.shape, BF),
            pltpu.VMEM(wo.shape, BF),
            pltpu.VMEM((rows, 2 * width), F32),
            *[pltpu.VMEM(s, t) for s, t in shapes],
            pltpu.SemaphoreType.DMA((5,)),
            pltpu.SemaphoreType.DMA((4,)),
            pltpu.SemaphoreType.DMA((2, units)),
        ],
        name="pair_core",
        compiler_params=pltpu.CompilerParams(vmem_limit_bytes=56 * 1024 * 1024),
    )(*ins)
    if positive:
        return [result[0], source] + list(result[1:])
    return result


def give_kernel(wanted, images, first, second):
    for p in range(first.shape[0] // 16):
        for s, out in enumerate((first, second)):
            at = jnp.maximum(wanted[p, s] - 1, 0)
            out[p * 16 : p * 16 + 16, :] = images[pl.ds(pl.multiple_of(at * 16, 16), 16), :]


def give(wanted, images):
    vm = pl.BlockSpec(memory_space=pltpu.VMEM)
    shape = jax.ShapeDtypeStruct((wanted.shape[0] * 16, images.shape[1]), BF)
    return pl.pallas_call(
        give_kernel,
        out_shape=[shape, shape],
        in_specs=[pl.BlockSpec(memory_space=pltpu.SMEM), vm],
        out_specs=[vm, vm],
        name="give",
    )(wanted, images)


def receive_kernel(wanted, own, first, second, out, total):
    total[...] = own[...]
    for s, part in enumerate((first, second)):

        def add(p, carry):
            at = wanted[p, s]

            @pl.when(at > 0)
            def _():
                rows = pl.ds(pl.multiple_of((at - 1) * 16, 16), 16)
                src = part[pl.ds(pl.multiple_of(p * 16, 16), 16), :]
                total[rows, :] = total[rows, :] + src.astype(F32)

            return carry

        lax.fori_loop(0, first.shape[0] // 16, add, 0)
    out[...] = total[...].astype(BF)


def receive(wanted, own, first, second):
    vm = pl.BlockSpec(memory_space=pltpu.VMEM)
    return pl.pallas_call(
        receive_kernel,
        out_shape=jax.ShapeDtypeStruct(own.shape, BF),
        in_specs=[pl.BlockSpec(memory_space=pltpu.SMEM), vm, vm, vm],
        out_specs=vm,
        scratch_shapes=[pltpu.VMEM(own.shape, F32)],
        name="receive",
        compiler_params=pltpu.CompilerParams(vmem_limit_bytes=56 * 1024 * 1024),
    )(wanted, own, first, second)


def route_kernel(named, wanted, owners, color0):
    count = named.shape[0]
    n = 2 * count
    peers = wanted.shape[0]
    o0, o1 = named[:, 0:1], named[:, 1:2]
    i = lax.broadcasted_iota(jnp.int32, (n, n), 0)
    k = lax.broadcasted_iota(jnp.int32, (n, n), 1)
    i_swap = jnp.where(i < count, i + count, i - count)
    k_swap = jnp.where(k < count, k + count, k - count)

    def row_of(col):
        return jnp.sum(jnp.where(i == k, col, 0), axis=0, keepdims=True)

    owner_col = jnp.concatenate([o0, o1], axis=0)
    swap_col = jnp.concatenate([o1, o0], axis=0)
    owner_row = row_of(owner_col)
    swap_row = row_of(swap_col)
    slot_row = row_of(jnp.concatenate([named[:, 2:3], named[:, 3:4]], axis=0))
    ahead = (owner_col == swap_row) & (i != k_swap)
    behind = (owner_row == swap_col) & (k != i_swap)
    reach = jnp.where(ahead | behind | (i == k), 1.0, 0.0)
    span = 1
    while span < count:
        low = reach.astype(BF)
        reach = jnp.where(dot_nn(low, low) > 0.5, 1.0, 0.0)
        span *= 2
    near = reach > 0.5
    first_row = jnp.min(jnp.where(near, i, n), axis=0, keepdims=True)
    second_row = jnp.min(jnp.where(near, i_swap, n), axis=0, keepdims=True)
    color_row = jnp.where(first_row < second_row, 0, 1)
    peer = lax.broadcasted_iota(jnp.int32, (peers, n), 0)
    asked = []
    for s in range(2):
        hit = (owner_row == peer) & (color_row == s)
        asked.append(jnp.sum(jnp.where(hit, slot_row + 1, 0), axis=1, keepdims=True))
    wanted[...] = jnp.concatenate(asked, axis=1)
    own_color = color_row[:, :count]
    swapped = owner_row[:, count:]
    straight = owner_row[:, :count]
    color0[...] = own_color
    owners[...] = jnp.concatenate(
        [jnp.where(own_color == 0, straight, swapped), jnp.where(own_color == 0, swapped, straight)],
        axis=0,
    )


def route(owner, slot, peers):
    vm = pl.BlockSpec(memory_space=pltpu.VMEM)
    count = owner.shape[0]
    return pl.pallas_call(
        route_kernel,
        out_shape=[
            jax.ShapeDtypeStruct((peers, 2), jnp.int32),
            jax.ShapeDtypeStruct((2, count), jnp.int32),
            jax.ShapeDtypeStruct((1, count), jnp.int32),
        ],
        in_specs=[vm],
        out_specs=[vm, vm, vm],
        name="route",
    )(jnp.concatenate([owner, slot], axis=1))


def weight_kernel(core, *refs, size, groups, with_text):
    flips = (1, 0)
    xs = refs[:groups]
    ds = refs[groups : 2 * groups]
    rest = refs[2 * groups :]
    if with_text:
        text, dt = rest[:2]
        rest = rest[2:]
        lhs = xs + (text,)
    else:
        lhs = xs
    outs = rest[: len(flips)]
    turned = rest[len(flips) :]
    step = pl.program_id(0)
    rows_of, width = xs[0].shape
    half = width // 2
    per = width // 256
    block_rows = half // size
    for flip, out, hold in zip(flips, outs, turned):
        for part in range(2):

            @pl.when((step == 0) & ((core[0] + flip) % 2 == part))
            def _():
                col = 0
                for src in lhs:
                    for i in range(src.shape[0] // 128):
                        block = src[i * 128 : i * 128 + 128, part * half : (part + 1) * half]
                        hold[:, col : col + 128] = block.T
                        col += 128

        def columns(n, carry, more):
            cols = pl.ds(pl.multiple_of(n * 256, 256), 256)
            acc = dot_nn(hold[:, :rows_of], ds[0][:, cols])
            for g in range(1, groups):
                acc = acc + dot_nn(hold[:, g * rows_of : (g + 1) * rows_of], ds[g][:, cols])
            if more:
                acc = acc + dot_nn(hold[:, groups * rows_of :], dt[:, cols])
            low = acc.astype(BF)
            for p in range(size):
                to = ((p + size - core[1 + flip]) % size) * block_rows
                rows = pl.ds(pl.multiple_of(to, block_rows), block_rows)
                out[rows, cols] = low[p * block_rows : (p + 1) * block_rows]
            return carry

        if with_text:

            @pl.when(step == 0)
            def _():
                lax.fori_loop(0, per, functools.partial(columns, more=False), 0)

            @pl.when(step > 0)
            def _():
                lax.fori_loop(0, per, functools.partial(columns, more=True), 0)

        else:
            lax.fori_loop(0, per, functools.partial(columns, more=False), 0)


def weight_gradients(core, size, xs, ds, text, dt):
    flips = (1, 0)
    groups = len(xs)
    with_text = text is not None
    rows_of, width = xs[0].shape
    whole = lambda t: pl.BlockSpec(t.shape, lambda n, core: (0, 0))
    specs = [whole(x) for x in xs]
    specs += [pl.BlockSpec((rows_of, width), lambda n, core: (0, n)) for d in ds]
    arrays = [*xs, *ds]
    depth = groups * rows_of
    if with_text:
        arrays += [text, dt]
        specs.append(whole(text))
        specs.append(
            pl.BlockSpec((text.shape[0], width), lambda n, core: (0, jnp.maximum(n - 1, 0)))
        )
        depth += text.shape[0]
    half = width // 2
    return pl.pallas_call(
        functools.partial(weight_kernel, size=size, groups=groups, with_text=with_text),
        grid_spec=pltpu.PrefetchScalarGridSpec(
            num_scalar_prefetch=1,
            grid=(ds[0].shape[1] // width,),
            in_specs=specs,
            out_specs=[pl.BlockSpec((half, width), lambda n, core: (0, n))] * len(flips),
            scratch_shapes=[pltpu.VMEM((half, depth), BF)] * len(flips),
        ),
        out_shape=[jax.ShapeDtypeStruct((half, ds[0].shape[1]), BF)] * len(flips),
        name="weight_gradients",
        compiler_params=pltpu.CompilerParams(vmem_limit_bytes=56 * 1024 * 1024),
    )(core, *arrays)


def finish_kernel(at, *refs, count, factor):
    for p in range(count):

        @pl.when(pl.program_id(0) == p)
        def _():
            refs[-1][...] = refs[p][...].astype(F32) * factor


def finish(places, parts, rows, factor, before):
    n = len(parts)
    height, total = parts[0].shape
    steps = 2 if height % 32 == 0 else 1
    block = height // steps
    given = [] if before is None else [before]

    def source(p):
        last = steps - 1
        return lambda g, i, at: (jnp.where(g == p, i, jnp.where(g > p, last, 0)), 0)

    return pl.pallas_call(
        functools.partial(finish_kernel, count=n, factor=factor),
        grid_spec=pltpu.PrefetchScalarGridSpec(
            num_scalar_prefetch=1,
            grid=(n, steps),
            in_specs=[pl.BlockSpec((block, total), source(p)) for p in range(n)]
            + [pl.BlockSpec(memory_space=pl.ANY)] * len(given),
            out_specs=pl.BlockSpec((block, total), lambda g, i, at: (at[g] * steps + i, 0)),
        ),
        out_shape=jax.ShapeDtypeStruct((rows, total), F32),
        input_output_aliases={1 + n: 0} if given else {},
        name="finish",
        compiler_params=pltpu.CompilerParams(vmem_limit_bytes=60 * 1024 * 1024),
    )(places[0].reshape(1) if n == 1 else jnp.stack(places), *parts, *given)


def grid_of(mesh):
    flat = list(mesh.devices.flat)
    sizes = [len({d.coords[a] for d in flat}) for a in range(3)]
    dims, stride = [], 1
    for s in [len(flat) // (sizes[0] * sizes[1] * sizes[2])] + sizes:
        dims.append((stride, s))
        stride *= s
    return dims


def coord(dim):
    return (lax.axis_index("dp") // dim[0]) % dim[1]


def by_core(even, odd):
    if even == odd:
        return coord(even)
    return jnp.where(lax.axis_index("dp") % 2 == 0, coord(even), coord(odd))


def shifted(x, dims, k):
    n = lax.axis_size("dp")
    table = []
    for i in range(n):
        stride, size = dims[i % 2]
        c = (i // stride) % size
        table.append((i, i + ((c + k) % size - c) * stride))
    return lax.ppermute(x, "dp", table)


def total_of(terms):
    total = terms[0].astype(F32)
    for t in terms[1:]:
        total = total + t.astype(F32)
    return total


def scatter_ready(terms, dims):
    size = dims[0][1]
    split = [t.reshape((size, t.shape[0] // size) + t.shape[1:]) for t in terms]
    got = [
        shifted(total_of([t[k] for t in split]).astype(BF), dims, k) for k in range(1, size)
    ]
    return [t[0] for t in split] + got


def scatter_terms(terms, dims):
    size = dims[0][1]
    at = by_core(*dims)
    split = [t.reshape((size, t.shape[0] // size) + t.shape[1:]) for t in terms]
    pick = lambda k: [
        lax.dynamic_index_in_dim(t, (at + k) % size, 0, keepdims=False) for t in split
    ]
    got = [shifted(total_of(pick(k)).astype(BF), dims, k) for k in range(1, size)]
    return pick(0) + got


def gather_rows(x, dims):
    size = dims[0][1]
    at = by_core(*dims)
    if size == 2:
        got = shifted(x, dims, 1)
        low = at == 0
        return jnp.concatenate([jnp.where(low, x, got), jnp.where(low, got, x)], axis=0)
    out = jnp.zeros((size,) + x.shape, x.dtype)
    out = lax.dynamic_update_index_in_dim(out, x, at, 0)
    for k in range(1, size):
        out = lax.dynamic_update_index_in_dim(out, shifted(x, dims, k), (at - k) % size, 0)
    return out.reshape((size * x.shape[0],) + x.shape[1:])


def step(
    text_states,
    text_len,
    query_states,
    neg_owner,
    neg_slot,
    projection_weight,
    output_weight,
    ln_gain,
    ln_bias,
    itm_weight,
    itm_bias,
    *,
    dims,
):
    captions, text_rows, width = text_states.shape
    image_rows = query_states.shape[1]
    peers = lax.axis_size("dp")
    wanted, owners, color = route(neg_owner, neg_slot, peers)
    requested = lax.all_to_all(wanted, "dp", split_axis=0, concat_axis=0, tiled=True)

    def exchange(t):
        split = t.reshape(peers, 1, image_rows, width)
        moved = lax.all_to_all(split, "dp", split_axis=0, concat_axis=0, tiled=True)
        return moved.reshape(t.shape)

    text = text_states.reshape(captions * text_rows, width)
    own = query_states.reshape(captions * image_rows, width)
    outgoing = give(requested, own)
    fetched = []
    for s in range(2):
        fetched.append(exchange(outgoing[s]))
    text_kv = dot_nn(text, projection_weight[:, width:]).astype(BF)
    results = []
    returned = []
    dtext = None
    for s in range(3):
        result = pair_core(
            BF if s == 2 else F32,
            text_len,
            own if s == 0 else fetched[s - 1],
            projection_weight,
            text_kv,
            output_weight,
            ln_gain[None],
            ln_bias[None],
            itm_weight.T,
            itm_bias,
            dtext,
            None if s == 0 else owners[s - 1],
        )
        results.append(result)
        dtext = result[5]
        if s > 0:
            returned.append(exchange(result[6]))

    rows = [r[1] for r in results]
    core = coord(dims[0]).reshape(1)
    core_dims = (dims[0], dims[0])
    x_dim, y_dim, z_dim = dims[1:]
    mixed = x_dim[1] == y_dim[1]
    flat_first = (x_dim, y_dim) if mixed else (x_dim, x_dim)
    flat_second = (y_dim, x_dim) if mixed else (y_dim, y_dim)
    deep = (z_dim, z_dim)
    factor = 1.0 / (captions * peers)

    size = flat_first[0][1]
    at = by_core(*flat_first)
    other_at = by_core(flat_first[1], flat_first[0])
    deep_at = coord(z_dim)
    send_a, keep_a = weight_gradients(
        jnp.stack([core[0], deep_at, deep_at]),
        z_dim[1],
        [r[3] for r in results],
        [r[2] for r in results],
        None,
        None,
    )
    a = [keep_a, shifted(send_a, core_dims, 1)]
    dqs = [r[4] for r in results]
    send_b, keep_b = weight_gradients(
        jnp.stack([core[0], at, other_at]), size, rows, dqs, text, dtext
    )
    b = [keep_b, shifted(send_b, core_dims, 1)]
    grad_text = dot_nt(dtext, projection_weight[:, width:]).astype(BF)

    heads = [r[0][:, :2] for r in results]
    straight = color.reshape(captions, 1) == 0
    logits = jnp.stack(
        [
            heads[0],
            jnp.where(straight, heads[1], heads[2]),
            jnp.where(straight, heads[2], heads[1]),
        ],
        axis=1,
    )

    a = scatter_ready(a, deep)
    b = scatter_ready(b, flat_first)
    b = scatter_terms(b, flat_second)
    a = scatter_terms(a, flat_first)
    b = scatter_terms(b, deep)
    a = scatter_terms(a, flat_second)
    a = total_of(a).astype(BF)
    b = total_of(b).astype(BF)
    b = gather_rows(b, deep)
    a = gather_rows(a, flat_second)
    a = gather_rows(a, flat_first)
    b = gather_rows(b, flat_second)
    a = gather_rows(a, deep)
    other_a = shifted(a, core_dims, 1)
    pieces = [(core[0] * size + at, b)]
    pieces.append(((1 - core[0]) * size + other_at, shifted(b, core_dims, 1)))
    for k in range(1, size):
        got = shifted(b, flat_first, k)
        pieces.append((core[0] * size + (at - k) % size, got))
        got = shifted(got, core_dims, 1)
        pieces.append(((1 - core[0]) * size + (other_at - k) % size, got))
    grad_query = receive(requested, results[0][6], *returned)
    sum_qkv = None
    for place, piece in pieces:
        sum_qkv = finish([place], [piece], width, factor, sum_qkv)
    sum_out = finish([core[0]], [a], width, factor, None)
    sum_out = finish([1 - core[0]], [other_a], width, factor, sum_out)
    return (
        logits,
        grad_text.reshape(captions, text_rows, width),
        grad_query.reshape(captions, image_rows, width),
        sum_qkv,
        sum_out,
    )


def solution(mesh):
    dims = grid_of(mesh)
    placed = (
        P("dp", None, None),
        P("dp"),
        P("dp", None, None),
        P("dp", None),
        P("dp", None),
        P(),
        P(),
        P(),
        P(),
        P(),
        P(),
    )
    return jax.shard_map(
        functools.partial(step, dims=dims),
        mesh=mesh,
        in_specs=placed,
        out_specs=(P("dp", None, None), P("dp", None, None), P("dp", None, None), P(), P()),
        check_vma=False,
    )
```

```python
import functools
import jax
import jax.numpy as jnp
from jax import lax
from jax.experimental import pallas as pl
from jax.experimental.pallas import tpu as pltpu

from jax.sharding import PartitionSpec as P


BF = jnp.bfloat16
F32 = jnp.float32


def dot_nt(a, b):
    return lax.dot_general(a, b, (((1,), (1,)), ((), ())), preferred_element_type=F32)


def dot_nn(a, b):
    return lax.dot_general(a, b, (((1,), (0,)), ((), ())), preferred_element_type=F32)


def core_kernel(lens, source, w_h, tkv, wo_h, gain, bias, head_w, head_b, text_h, place, logits, x_h, ga_h, ctx_h, dqkv_h, dtext_h, back_h, qkv, probs, dctx, gh, w, wo, text_in, x, ga, ctx, dqkv, dtext, back, sem_in, sem_out, sem_rows, *, positive):
    rows, width = ctx.shape
    loads = [
        pltpu.make_async_copy(
            w_h.at[:, pl.ds(n * width, width)], w.at[:, pl.ds(n * width, width)], sem_in.at[n]
        )
        for n in range(3)
    ]
    loads.append(pltpu.make_async_copy(wo_h, wo, sem_in.at[3]))
    if not positive:
        loads.append(pltpu.make_async_copy(text_h, text_in, sem_in.at[4]))
    loads[0].start()
    loads[1].start()
    saves = []

    def save(src, dst):
        copy = pltpu.make_async_copy(src, dst, sem_out.at[len(saves)])
        copy.start()
        saves.append(copy)

    pairs_of_units = rows // 64
    quads = width // 256
    scale = 0.125
    lane = lax.broadcasted_iota(jnp.int32, (128, 128), 1)
    left = lane < 64
    lane32 = lax.broadcasted_iota(jnp.int32, (32, 128), 1)
    row32 = lax.broadcasted_iota(jnp.int32, (32, 128), 0)
    qg = row32 // 16
    uu = lane32 // 64
    key = lane32 % 64
    is_image = key < 32
    image_ok = is_image & ((key // 16) == qg)
    tg = (key - 32) // 16
    tpos = key % 16
    text_ok = jnp.logical_not(is_image) & (tg == qg)
    half32 = lane32 < 64
    hm_lane = lax.broadcasted_iota(jnp.int32, (1, 256), 1) // 64
    head_mask = [(hm_lane == h).astype(F32).astype(BF) for h in range(4)]
    zero64 = jnp.zeros((64, 256), BF)

    def head_blocks(t):
        return jnp.concatenate([t * m for m in head_mask], axis=0)

    def unit_rows(j, u):
        return pl.ds(pl.multiple_of(j * 64 + u * 32, 32), 32)

    def stacked(j, part, q):
        cols = pl.ds(width * part + q * 256, 256)
        tcols = pl.ds(width * (part - 1) + q * 256, 256)
        both = []
        for u in range(2):
            t = jnp.concatenate([qkv[unit_rows(j, u), cols], tkv[unit_rows(j, u), tcols]], axis=0)
            both.append(t)
        return jnp.concatenate(
            [jnp.concatenate([both[0], zero64], axis=1), jnp.concatenate([zero64, both[1]], axis=1)],
            axis=0,
        )

    def wide(ref, j, q):
        cols = pl.ds(q * 256, 256)
        return [head_blocks(ref[unit_rows(j, u), cols]) for u in range(2)]

    def gathered(full, u):
        parts = []
        for t in range(2):
            cols = slice(u * 256 + t * 128, u * 256 + t * 128 + 128)
            a = full[(2 * t) * 32 : (2 * t + 1) * 32, cols]
            b = full[(2 * t + 1) * 32 : (2 * t + 2) * 32, cols]
            parts.append(jnp.where(half32, a, b))
        return jnp.concatenate(parts, axis=1)

    def half_reduce(t, fill, op):
        a = op(jnp.where(left, t, fill), axis=1, keepdims=True)
        b = op(jnp.where(left, fill, t), axis=1, keepdims=True)
        return a, b

    def forward(j, carry):
        n = [lens[4 * j + i] for i in range(4)]
        limit = jnp.where(
            uu == 0, jnp.where(qg == 0, n[0], n[1]), jnp.where(qg == 0, n[2], n[3])
        )
        valid32 = image_ok | (text_ok & (tpos < limit))
        valid32 = jnp.where(valid32, 1.0, 0.0)
        valid = jnp.concatenate([valid32] * 4, axis=0) > 0.5
        for q in range(quads):
            queries = wide(qkv, j, q)
            keys = stacked(j, 1, q)
            s = dot_nt(jnp.concatenate(queries, axis=1), keys) * scale
            s = jnp.where(valid, s, -1e30)
            m0, m1 = half_reduce(s, -3e38, jnp.max)
            e = jnp.exp(s - jnp.where(left, m0, m1))
            d0, d1 = half_reduce(e, 0.0, jnp.sum)
            p = e * jnp.where(left, 1.0 / d0, 1.0 / d1)
            probs[j, q] = p
            full = dot_nn(p.astype(BF), stacked(j, 2, q))
            for u in range(2):
                ctx[unit_rows(j, u), pl.ds(q * 256, 256)] = gathered(full, u).astype(BF)
        return carry

    if positive:
        x = source
    else:
        for i in range(rows // 16):
            x[i * 16 : i * 16 + 16, :] = source[pl.ds(pl.multiple_of(place[i] * 16, 16), 16), :]
        save(x, x_h)

    def project(n, carry):
        cols = pl.ds(pl.multiple_of(n * 256, 256), 256)
        qkv[:, cols] = dot_nn(x[...], w[:, cols]).astype(BF)
        return carry

    per = width // 256
    for n in range(3):
        loads[n].wait()
        for load in loads[2:3] if n == 0 else loads[3:] if n == 1 else []:
            load.start()
        lax.fori_loop(n * per, (n + 1) * per, project, 0, unroll=3)
    lax.fori_loop(0, pairs_of_units, forward, 0, unroll=4)
    save(ctx, ctx_h)
    loads[3].wait()

    chunk = 128
    w0 = head_w[0:1, :]
    w1 = head_w[1:2, :]

    def middle(i, carry):
        rs = pl.ds(pl.multiple_of(i * chunk, chunk), chunk)
        hid = x[rs, :].astype(F32) + dot_nn(ctx[rs, :], wo[...])
        cen = hid - jnp.mean(hid, axis=1, keepdims=True)
        spread = jnp.mean(cen * cen, axis=1, keepdims=True)
        inv = lax.rsqrt(spread + 1e-06)
        xhat = cen * inv
        pooled = jnp.sum(xhat.reshape(chunk // 16, 16, width), axis=1) * (1.0 / 16.0)
        pooled = pooled * gain[...] + bias[...]
        l0 = jnp.sum(pooled * w0, axis=1, keepdims=True) + head_b[0]
        l1 = jnp.sum(pooled * w1, axis=1, keepdims=True) + head_b[1]
        cols = lax.broadcasted_iota(jnp.int32, (chunk // 16, 128), 1)
        logits[pl.ds(pl.multiple_of(i * (chunk // 16), chunk // 16), chunk // 16), :] = jnp.where(
            cols == 0, l0, l1
        )
        top = jnp.maximum(l0, l1)
        e0 = jnp.exp(l0 - top)
        e1 = jnp.exp(l1 - top)
        wrong = (e0 if positive else e1) / (e0 + e1)
        slope = (w0 - w1) if positive else (w1 - w0)
        dx = (wrong * (1.0 / 16.0)) * slope * gain[...]
        mean_dx = jnp.mean(dx, axis=1, keepdims=True)
        dx = jnp.broadcast_to(dx[:, None, :], (chunk // 16, 16, width)).reshape(chunk, width)
        mean_dx = jnp.broadcast_to(mean_dx[:, None, :], (chunk // 16, 16, 1)).reshape(chunk, 1)
        along = jnp.mean(dx * xhat, axis=1, keepdims=True)
        g = inv * (dx - mean_dx - xhat * along)
        gh[rs, :] = g
        gl = g.astype(BF)
        ga[rs, :] = gl
        dctx[rs, :] = dot_nt(gl, wo[...]).astype(BF)
        return carry

    lax.fori_loop(0, rows // chunk, middle, 0, unroll=2)
    save(ga, ga_h)
    if not positive:
        loads[4].wait()

    def row_copies(j):
        rs = pl.ds(pl.multiple_of(j * 64, 64), 64)
        return [
            pltpu.make_async_copy(dqkv.at[rs, :], dqkv_h.at[rs, :], sem_rows.at[0, j]),
            pltpu.make_async_copy(dtext.at[rs, :], dtext_h.at[rs, :], sem_rows.at[1, j]),
        ]

    def backward(j, carry):
        for q in range(quads):
            p = probs[j, q]
            dc = wide(dctx, j, q)
            dp = dot_nt(jnp.concatenate(dc, axis=1), stacked(j, 2, q))
            r0, r1 = half_reduce(dp * p, 0.0, jnp.sum)
            ds = (p * (dp - jnp.where(left, r0, r1)) * scale).astype(BF)
            full = dot_nn(ds, stacked(j, 1, q))
            for u in range(2):
                dqkv[unit_rows(j, u), pl.ds(q * 256, 256)] = gathered(full, u).astype(BF)
            queries = wide(qkv, j, q)
            dst = ds.T
            pt = p.astype(BF).T
            for part, lhs, rhs in ((1, dst, queries), (2, pt, dc)):
                outs = [dot_nn(lhs[u * 64 : u * 64 + 64], rhs[u]) for u in range(2)]
                for u in range(2):
                    dqkv[unit_rows(j, u), pl.ds(width * part + q * 256, 256)] = outs[u][:32].astype(BF)
                tcols = pl.ds(width * (part - 1) + q * 256, 256)
                for u in range(2):
                    total = outs[u][32:]
                    if not positive:
                        total = total + text_in[unit_rows(j, u), tcols]
                    dtext[unit_rows(j, u), tcols] = total.astype(dtext.dtype)
        for copy in row_copies(j):
            copy.start()
        return carry

    lax.fori_loop(0, pairs_of_units, backward, 0, unroll=2)

    def images(n, carry):
        cols = pl.ds(pl.multiple_of(n * 256, 256), 256)
        g = dot_nt(dqkv[...], w[cols, :]) + gh[:, cols]
        if positive:
            back[:, cols] = g
        else:
            gh[:, cols] = g
        return carry

    lax.fori_loop(0, width // 256, images, 0, unroll=3)
    if not positive:
        back[...] = jnp.zeros(back.shape, BF)
        for i in range(rows // 16):
            at = pl.ds(pl.multiple_of(place[i] * 16, 16), 16)
            back[at, :] = gh[i * 16 : i * 16 + 16, :].astype(BF)
    save(back, back_h)
    for j in range(pairs_of_units):
        for copy in row_copies(j):
            copy.wait()
    for copy in saves:
        copy.wait()


def pair_core(text_type, lens, source, w, tkv, wo, gain, bias, head_w, head_b, text_in, place):
    rows, width = tkv.shape[0], wo.shape[0]
    positive = place is None
    vm = pl.BlockSpec(memory_space=pltpu.VMEM)
    sm = pl.BlockSpec(memory_space=pltpu.SMEM)
    far = pl.BlockSpec(memory_space=pl.ANY)
    ins = [lens, source, w, tkv, wo, gain, bias, head_w, head_b]
    specs = [sm, vm, far, vm, far, vm, vm, vm, sm]
    if not positive:
        ins += [text_in, place]
        specs += [far, sm]
    back_type = F32 if positive else BF
    shapes = [
        ((rows, width), BF),
        ((rows, width), BF),
        ((rows, width), BF),
        ((rows, 3 * width), BF),
        ((rows, 2 * width), text_type),
        (source.shape, back_type),
    ]
    out = [jax.ShapeDtypeStruct((rows // 16, 128), F32)]
    out += [jax.ShapeDtypeStruct(s, t) for s, t in shapes]
    if positive:
        del out[1]

    def body(*refs):
        if positive:
            refs = refs[:9] + (None, None, refs[9], None) + refs[10:]
        core_kernel(*refs, positive=positive)

    units = rows // 64
    result = pl.pallas_call(
        body,
        out_shape=out,
        in_specs=specs,
        out_specs=[vm] + [far] * (len(out) - 1),
        scratch_shapes=[
            pltpu.VMEM((rows, 3 * width), BF),
            pltpu.VMEM((units, width // 256, 128, 128), F32),
            pltpu.VMEM((rows, width), BF),
            pltpu.VMEM((rows, width), F32),
            pltpu.VMEM(w.shape, BF),
            pltpu.VMEM(wo.shape, BF),
            pltpu.VMEM((rows, 2 * width), F32),
            *[pltpu.VMEM(s, t) for s, t in shapes],
            pltpu.SemaphoreType.DMA((5,)),
            pltpu.SemaphoreType.DMA((4,)),
            pltpu.SemaphoreType.DMA((2, units)),
        ],
        name="pair_core",
        compiler_params=pltpu.CompilerParams(vmem_limit_bytes=56 * 1024 * 1024),
    )(*ins)
    if positive:
        return [result[0], source] + list(result[1:])
    return result


def give_kernel(wanted, images, first, second):
    for p in range(first.shape[0] // 16):
        for s, out in enumerate((first, second)):
            at = jnp.maximum(wanted[p, s] - 1, 0)
            out[p * 16 : p * 16 + 16, :] = images[pl.ds(pl.multiple_of(at * 16, 16), 16), :]


def give(wanted, images):
    vm = pl.BlockSpec(memory_space=pltpu.VMEM)
    shape = jax.ShapeDtypeStruct((wanted.shape[0] * 16, images.shape[1]), BF)
    return pl.pallas_call(
        give_kernel,
        out_shape=[shape, shape],
        in_specs=[pl.BlockSpec(memory_space=pltpu.SMEM), vm],
        out_specs=[vm, vm],
        name="give",
    )(wanted, images)


def receive_kernel(wanted, own, first, second, out, total):
    total[...] = own[...]
    for s, part in enumerate((first, second)):

        def add(p, carry):
            at = wanted[p, s]

            @pl.when(at > 0)
            def _():
                rows = pl.ds(pl.multiple_of((at - 1) * 16, 16), 16)
                src = part[pl.ds(pl.multiple_of(p * 16, 16), 16), :]
                total[rows, :] = total[rows, :] + src.astype(F32)

            return carry

        lax.fori_loop(0, first.shape[0] // 16, add, 0)
    out[...] = total[...].astype(BF)


def receive(wanted, own, first, second):
    vm = pl.BlockSpec(memory_space=pltpu.VMEM)
    return pl.pallas_call(
        receive_kernel,
        out_shape=jax.ShapeDtypeStruct(own.shape, BF),
        in_specs=[pl.BlockSpec(memory_space=pltpu.SMEM), vm, vm, vm],
        out_specs=vm,
        scratch_shapes=[pltpu.VMEM(own.shape, F32)],
        name="receive",
        compiler_params=pltpu.CompilerParams(vmem_limit_bytes=56 * 1024 * 1024),
    )(wanted, own, first, second)


def route_kernel(named, wanted, owners, color0):
    count = named.shape[0]
    n = 2 * count
    peers = wanted.shape[0]
    o0, o1 = named[:, 0:1], named[:, 1:2]
    i = lax.broadcasted_iota(jnp.int32, (n, n), 0)
    k = lax.broadcasted_iota(jnp.int32, (n, n), 1)
    i_swap = jnp.where(i < count, i + count, i - count)
    k_swap = jnp.where(k < count, k + count, k - count)

    def row_of(col):
        return jnp.sum(jnp.where(i == k, col, 0), axis=0, keepdims=True)

    owner_col = jnp.concatenate([o0, o1], axis=0)
    swap_col = jnp.concatenate([o1, o0], axis=0)
    owner_row = row_of(owner_col)
    swap_row = row_of(swap_col)
    slot_row = row_of(jnp.concatenate([named[:, 2:3], named[:, 3:4]], axis=0))
    ahead = (owner_col == swap_row) & (i != k_swap)
    behind = (owner_row == swap_col) & (k != i_swap)
    reach = jnp.where(ahead | behind | (i == k), 1.0, 0.0)
    span = 1
    while span < count:
        low = reach.astype(BF)
        reach = jnp.where(dot_nn(low, low) > 0.5, 1.0, 0.0)
        span *= 2
    near = reach > 0.5
    first_row = jnp.min(jnp.where(near, i, n), axis=0, keepdims=True)
    second_row = jnp.min(jnp.where(near, i_swap, n), axis=0, keepdims=True)
    color_row = jnp.where(first_row < second_row, 0, 1)
    peer = lax.broadcasted_iota(jnp.int32, (peers, n), 0)
    asked = []
    for s in range(2):
        hit = (owner_row == peer) & (color_row == s)
        asked.append(jnp.sum(jnp.where(hit, slot_row + 1, 0), axis=1, keepdims=True))
    wanted[...] = jnp.concatenate(asked, axis=1)
    own_color = color_row[:, :count]
    swapped = owner_row[:, count:]
    straight = owner_row[:, :count]
    color0[...] = own_color
    owners[...] = jnp.concatenate(
        [jnp.where(own_color == 0, straight, swapped), jnp.where(own_color == 0, swapped, straight)],
        axis=0,
    )


def route(owner, slot, peers):
    vm = pl.BlockSpec(memory_space=pltpu.VMEM)
    count = owner.shape[0]
    return pl.pallas_call(
        route_kernel,
        out_shape=[
            jax.ShapeDtypeStruct((peers, 2), jnp.int32),
            jax.ShapeDtypeStruct((2, count), jnp.int32),
            jax.ShapeDtypeStruct((1, count), jnp.int32),
        ],
        in_specs=[vm],
        out_specs=[vm, vm, vm],
        name="route",
    )(jnp.concatenate([owner, slot], axis=1))


def weight_kernel(core, *refs, size, groups, with_text):
    flips = (1, 0)
    xs = refs[:groups]
    ds = refs[groups : 2 * groups]
    rest = refs[2 * groups :]
    if with_text:
        text, dt = rest[:2]
        rest = rest[2:]
        lhs = xs + (text,)
    else:
        lhs = xs
    outs = rest[: len(flips)]
    turned = rest[len(flips) :]
    step = pl.program_id(0)
    rows_of, width = xs[0].shape
    half = width // 2
    per = width // 256
    block_rows = half // size
    for flip, out, hold in zip(flips, outs, turned):
        for part in range(2):

            @pl.when((step == 0) & ((core[0] + flip) % 2 == part))
            def _():
                col = 0
                for src in lhs:
                    for i in range(src.shape[0] // 128):
                        block = src[i * 128 : i * 128 + 128, part * half : (part + 1) * half]
                        hold[:, col : col + 128] = block.T
                        col += 128

        def columns(n, carry, more):
            cols = pl.ds(pl.multiple_of(n * 256, 256), 256)
            acc = dot_nn(hold[:, :rows_of], ds[0][:, cols])
            for g in range(1, groups):
                acc = acc + dot_nn(hold[:, g * rows_of : (g + 1) * rows_of], ds[g][:, cols])
            if more:
                acc = acc + dot_nn(hold[:, groups * rows_of :], dt[:, cols])
            low = acc.astype(BF)
            for p in range(size):
                to = ((p + size - core[1 + flip]) % size) * block_rows
                rows = pl.ds(pl.multiple_of(to, block_rows), block_rows)
                out[rows, cols] = low[p * block_rows : (p + 1) * block_rows]
            return carry

        if with_text:

            @pl.when(step == 0)
            def _():
                lax.fori_loop(0, per, functools.partial(columns, more=False), 0)

            @pl.when(step > 0)
            def _():
                lax.fori_loop(0, per, functools.partial(columns, more=True), 0)

        else:
            lax.fori_loop(0, per, functools.partial(columns, more=False), 0)


def weight_gradients(core, size, xs, ds, text, dt):
    flips = (1, 0)
    groups = len(xs)
    with_text = text is not None
    rows_of, width = xs[0].shape
    whole = lambda t: pl.BlockSpec(t.shape, lambda n, core: (0, 0))
    specs = [whole(x) for x in xs]
    specs += [pl.BlockSpec((rows_of, width), lambda n, core: (0, n)) for d in ds]
    arrays = [*xs, *ds]
    depth = groups * rows_of
    if with_text:
        arrays += [text, dt]
        specs.append(whole(text))
        specs.append(
            pl.BlockSpec((text.shape[0], width), lambda n, core: (0, jnp.maximum(n - 1, 0)))
        )
        depth += text.shape[0]
    half = width // 2
    return pl.pallas_call(
        functools.partial(weight_kernel, size=size, groups=groups, with_text=with_text),
        grid_spec=pltpu.PrefetchScalarGridSpec(
            num_scalar_prefetch=1,
            grid=(ds[0].shape[1] // width,),
            in_specs=specs,
            out_specs=[pl.BlockSpec((half, width), lambda n, core: (0, n))] * len(flips),
            scratch_shapes=[pltpu.VMEM((half, depth), BF)] * len(flips),
        ),
        out_shape=[jax.ShapeDtypeStruct((half, ds[0].shape[1]), BF)] * len(flips),
        name="weight_gradients",
        compiler_params=pltpu.CompilerParams(vmem_limit_bytes=56 * 1024 * 1024),
    )(core, *arrays)


def finish_kernel(at, *refs, count, factor):
    for p in range(count):

        @pl.when(pl.program_id(0) == p)
        def _():
            refs[-1][...] = refs[p][...].astype(F32) * factor


def finish(places, parts, rows, factor, before):
    n = len(parts)
    height, total = parts[0].shape
    steps = 2 if height % 32 == 0 else 1
    block = height // steps
    given = [] if before is None else [before]

    def source(p):
        last = steps - 1
        return lambda g, i, at: (jnp.where(g == p, i, jnp.where(g > p, last, 0)), 0)

    return pl.pallas_call(
        functools.partial(finish_kernel, count=n, factor=factor),
        grid_spec=pltpu.PrefetchScalarGridSpec(
            num_scalar_prefetch=1,
            grid=(n, steps),
            in_specs=[pl.BlockSpec((block, total), source(p)) for p in range(n)]
            + [pl.BlockSpec(memory_space=pl.ANY)] * len(given),
            out_specs=pl.BlockSpec((block, total), lambda g, i, at: (at[g] * steps + i, 0)),
        ),
        out_shape=jax.ShapeDtypeStruct((rows, total), F32),
        input_output_aliases={1 + n: 0} if given else {},
        name="finish",
        compiler_params=pltpu.CompilerParams(vmem_limit_bytes=60 * 1024 * 1024),
    )(places[0].reshape(1) if n == 1 else jnp.stack(places), *parts, *given)


def grid_of(mesh):
    flat = list(mesh.devices.flat)
    sizes = [len({d.coords[a] for d in flat}) for a in range(3)]
    dims, stride = [], 1
    for s in [len(flat) // (sizes[0] * sizes[1] * sizes[2])] + sizes:
        dims.append((stride, s))
        stride *= s
    return dims


def coord(dim):
    return (lax.axis_index("dp") // dim[0]) % dim[1]


def by_core(even, odd):
    if even == odd:
        return coord(even)
    return jnp.where(lax.axis_index("dp") % 2 == 0, coord(even), coord(odd))


def shifted(x, dims, k):
    n = lax.axis_size("dp")
    table = []
    for i in range(n):
        stride, size = dims[i % 2]
        c = (i // stride) % size
        table.append((i, i + ((c + k) % size - c) * stride))
    return lax.ppermute(x, "dp", table)


def total_of(terms):
    total = terms[0].astype(F32)
    for t in terms[1:]:
        total = total + t.astype(F32)
    return total


def scatter_ready(terms, dims):
    size = dims[0][1]
    split = [t.reshape((size, t.shape[0] // size) + t.shape[1:]) for t in terms]
    got = [
        shifted(total_of([t[k] for t in split]).astype(BF), dims, k) for k in range(1, size)
    ]
    return [t[0] for t in split] + got


def scatter_terms(terms, dims):
    size = dims[0][1]
    at = by_core(*dims)
    split = [t.reshape((size, t.shape[0] // size) + t.shape[1:]) for t in terms]
    pick = lambda k: [
        lax.dynamic_index_in_dim(t, (at + k) % size, 0, keepdims=False) for t in split
    ]
    got = [shifted(total_of(pick(k)).astype(BF), dims, k) for k in range(1, size)]
    return pick(0) + got


def gather_rows(x, dims):
    size = dims[0][1]
    at = by_core(*dims)
    if size == 2:
        got = shifted(x, dims, 1)
        low = at == 0
        return jnp.concatenate([jnp.where(low, x, got), jnp.where(low, got, x)], axis=0)
    out = jnp.zeros((size,) + x.shape, x.dtype)
    out = lax.dynamic_update_index_in_dim(out, x, at, 0)
    for k in range(1, size):
        out = lax.dynamic_update_index_in_dim(out, shifted(x, dims, k), (at - k) % size, 0)
    return out.reshape((size * x.shape[0],) + x.shape[1:])


def step(
    text_states,
    text_len,
    query_states,
    neg_owner,
    neg_slot,
    projection_weight,
    output_weight,
    ln_gain,
    ln_bias,
    itm_weight,
    itm_bias,
    *,
    dims,
):
    captions, text_rows, width = text_states.shape
    image_rows = query_states.shape[1]
    peers = lax.axis_size("dp")
    wanted, owners, color = route(neg_owner, neg_slot, peers)
    requested = lax.all_to_all(wanted, "dp", split_axis=0, concat_axis=0, tiled=True)

    def exchange(t):
        split = t.reshape(peers, 1, image_rows, width)
        moved = lax.all_to_all(split, "dp", split_axis=0, concat_axis=0, tiled=True)
        return moved.reshape(t.shape)

    text = text_states.reshape(captions * text_rows, width)
    own = query_states.reshape(captions * image_rows, width)
    outgoing = give(requested, own)
    fetched = []
    for s in range(2):
        fetched.append(exchange(outgoing[s]))
    text_kv = dot_nn(text, projection_weight[:, width:]).astype(BF)
    results = []
    returned = []
    dtext = None
    for s in range(3):
        result = pair_core(
            BF if s == 2 else F32,
            text_len,
            own if s == 0 else fetched[s - 1],
            projection_weight,
            text_kv,
            output_weight,
            ln_gain[None],
            ln_bias[None],
            itm_weight.T,
            itm_bias,
            dtext,
            None if s == 0 else owners[s - 1],
        )
        results.append(result)
        dtext = result[5]
        if s > 0:
            returned.append(exchange(result[6]))

    rows = [r[1] for r in results]
    core = coord(dims[0]).reshape(1)
    core_dims = (dims[0], dims[0])
    x_dim, y_dim, z_dim = dims[1:]
    mixed = x_dim[1] == y_dim[1]
    flat_first = (x_dim, y_dim) if mixed else (x_dim, x_dim)
    flat_second = (y_dim, x_dim) if mixed else (y_dim, y_dim)
    deep = (z_dim, z_dim)
    factor = 1.0 / (captions * peers)

    size = flat_first[0][1]
    at = by_core(*flat_first)
    other_at = by_core(flat_first[1], flat_first[0])
    deep_at = coord(z_dim)
    send_a, keep_a = weight_gradients(
        jnp.stack([core[0], deep_at, deep_at]),
        z_dim[1],
        [r[3] for r in results],
        [r[2] for r in results],
        None,
        None,
    )
    a = [keep_a, shifted(send_a, core_dims, 1)]
    dqs = [r[4] for r in results]
    send_b, keep_b = weight_gradients(
        jnp.stack([core[0], at, other_at]), size, rows, dqs, text, dtext
    )
    b = [keep_b, shifted(send_b, core_dims, 1)]
    grad_text = dot_nt(dtext, projection_weight[:, width:]).astype(BF)

    heads = [r[0][:, :2] for r in results]
    straight = color.reshape(captions, 1) == 0
    logits = jnp.stack(
        [
            heads[0],
            jnp.where(straight, heads[1], heads[2]),
            jnp.where(straight, heads[2], heads[1]),
        ],
        axis=1,
    )

    a = scatter_ready(a, deep)
    b = scatter_ready(b, flat_first)
    b = scatter_terms(b, flat_second)
    a = scatter_terms(a, flat_first)
    b = scatter_terms(b, deep)
    a = scatter_terms(a, flat_second)
    a = total_of(a).astype(BF)
    b = total_of(b).astype(BF)
    b = gather_rows(b, deep)
    a = gather_rows(a, flat_second)
    a = gather_rows(a, flat_first)
    b = gather_rows(b, flat_second)
    a = gather_rows(a, deep)
    other_a = shifted(a, core_dims, 1)
    pieces = [(core[0] * size + at, b)]
    pieces.append(((1 - core[0]) * size + other_at, shifted(b, core_dims, 1)))
    for k in range(1, size):
        got = shifted(b, flat_first, k)
        pieces.append((core[0] * size + (at - k) % size, got))
        got = shifted(got, core_dims, 1)
        pieces.append(((1 - core[0]) * size + (other_at - k) % size, got))
    grad_query = receive(requested, results[0][6], *returned)
    sum_qkv = None
    for i, (place, piece) in enumerate(pieces):
        if i == 0:
            sum_qkv = finish([place], [piece], width, factor, None)
        else:
            scaled = piece.astype(F32) * factor
            sum_qkv = lax.dynamic_update_slice(sum_qkv, scaled, (place * piece.shape[0], 0))
    sum_out = finish([core[0]], [a], width, factor, None)
    scaled = other_a.astype(F32) * factor
    sum_out = lax.dynamic_update_slice(sum_out, scaled, ((1 - core[0]) * a.shape[0], 0))
    return (
        logits,
        grad_text.reshape(captions, text_rows, width),
        grad_query.reshape(captions, image_rows, width),
        sum_qkv,
        sum_out,
    )


def solution(mesh):
    dims = grid_of(mesh)
    placed = (
        P("dp", None, None),
        P("dp"),
        P("dp", None, None),
        P("dp", None),
        P("dp", None),
        P(),
        P(),
        P(),
        P(),
        P(),
        P(),
    )
    return jax.shard_map(
        functools.partial(step, dims=dims),
        mesh=mesh,
        in_specs=placed,
        out_specs=(P("dp", None, None), P("dp", None, None), P("dp", None, None), P(), P()),
        check_vma=False,
    )
```
